256 devices in a mesh: segment: 2 (over x_lo), seq: 16 (over y, x_hi, core), mp: 8 (over z).
Axes of the slice: x: 4 (x_hi: 2, x_lo: 2; x = x_hi * 2 + x_lo), y: 4, z: 8, core: 2. Of those that a mesh axis runs over, the one named last changes fastest.
Arguments:
- enc_states: bfloat16 [4096, 4096], P('seq', 'mp'), may hold values from -6 to 6
- dec_states: bfloat16 [4096, 4096], P('seq', 'mp'), may hold values from -21 to 21
- section_weights: bfloat16 [2, 4096, 2, 4096], P('segment', None, None, 'mp'), may hold values from -3 to 3
- group_lengths: int32 [32], P('seq'), may hold values from 1 to 128, 3072 in all
Outputs:
- mixed: bfloat16 [4096, 4096], P('seq', ('segment', 'mp'))
The draws below stay inside these ranges and needn't reach their ends.
Inputs may be any that keep to these rules, and one draw needn't show every extreme that they name: Rows c * 128 to c * 128 + group_lengths[c] - 1 of the memory are real, the rest of block c is padding.
All inputs are finite; a program needn't handle non-finite values.
Results may differ from the reference program's by a relative error of at most 0.018.
Values may be sent and summed in bfloat16 or wider, within the bound.
A program may use at most 128 MiB of HBM per device.

```python
import math
import jax
import jax.numpy as jnp
import numpy as np
from jax import lax

D = 4096
HEADS = 16
DH = 256
GROUP = 128
ENC_ROWS = 4096
DEC_ROWS = 4096
GROUPS = 32


def encoder_values(key):
    inner = jax.random.fold_in(key, 11)
    values = jnp.clip(jax.random.normal(inner, (ENC_ROWS, D), jnp.float32), -6.0, 6.0)
    return values


def draw_enc_states(key, part):
    return encoder_values(key).astype(jnp.bfloat16)


def draw_dec_states(key, part):
    inner = jax.random.fold_in(key, 23)
    values = jnp.clip(jax.random.normal(inner, (DEC_ROWS, D), jnp.float32), -6.0, 6.0)
    return values.astype(jnp.bfloat16)


def draw_section_weights(key, part):
    inner = jax.random.fold_in(key, 37)
    factor = D ** (-0.5)
    values = jnp.clip(jax.random.normal(inner, (2, D, 2, D), jnp.float32), -6.0, 6.0) * factor
    values = values.at[1, :, 0, :].multiply(3.0)
    return values.astype(jnp.bfloat16)


def profile(number_of, total, reach, lean):
    weights = [(1 << 20) // math.isqrt(grade ** lean) + 1 for grade in range(2, number_of + 1)]
    surplus, given = total - reach - (number_of - 1), [1] * (number_of - 1)
    while surplus > 0:
        free = [i for i in range(number_of - 1) if given[i] < reach]
        mass, budget = sum([weights[i] for i in free]), surplus
        for i in free:
            addition = min(reach - given[i], max(1, budget * weights[i] // mass), surplus)
            given[i] = given[i] + addition
            surplus = surplus - addition
    return np.array([reach] + given)


def uneven_parts(stream_key, amount, total, most, lean):
    if amount == 2:
        one = jax.random.randint(stream_key, (), max(1, total - most), min(most, total - 1) + 1)
        return jnp.stack([one, total - one])
    tallies = jnp.asarray(profile(amount, total, most, lean), jnp.int32)
    twos = (amount - 1) // 2
    donor, taker = tallies[1:1 + 2 * twos:2], tallies[2:2 + 2 * twos:2]
    slack = jnp.minimum(donor - 1, most - taker)
    shifted = jax.random.randint(jax.random.fold_in(stream_key, 1), (twos,), 0, 1 << 20) % (slack + 1)
    tallies = tallies.at[1:1 + 2 * twos:2].set(donor - shifted).at[2:2 + 2 * twos:2].set(taker + shifted)
    return tallies[jax.random.permutation(jax.random.fold_in(stream_key, 2), amount)]


def setup_inputs(seed: int = 0) -> dict:
    streams_of = jax.random.split(jax.random.key(seed), 5)
    enc_states = draw_enc_states(jax.random.fold_in(streams_of[4], 71), 0)
    dec_states = draw_dec_states(jax.random.fold_in(streams_of[4], 71), 0)
    section_weights = draw_section_weights(jax.random.fold_in(streams_of[4], 71), 0)
    group_lengths = uneven_parts(streams_of[3], GROUPS, GROUPS * GROUP * 3 // 4, GROUP, 0).astype(jnp.int32)
    return {"enc_states": enc_states, "dec_states": dec_states, "section_weights": section_weights, "group_lengths": group_lengths}


def split_heads(matrix, rows):
    return matrix.reshape(rows, HEADS, DH).transpose(1, 0, 2)


def reference(enc_states, dec_states, section_weights, group_lengths):
    key_weight = section_weights[0, :, 0, :]
    value_weight = section_weights[0, :, 1, :]
    query_weight = section_weights[1, :, 0, :]
    output_weight = section_weights[1, :, 1, :]
    memory_keys = jnp.dot(enc_states, key_weight, preferred_element_type=jnp.float32).astype(jnp.bfloat16)
    memory_values = jnp.dot(enc_states, value_weight, preferred_element_type=jnp.float32).astype(jnp.bfloat16)
    queries = jnp.dot(dec_states, query_weight, preferred_element_type=jnp.float32).astype(jnp.bfloat16)
    valid = (jnp.arange(GROUP)[None, :] < group_lengths[:, None]).reshape(ENC_ROWS)
    scale = DH ** -0.5

    def one_head(operands):
        query_head, key_head, value_head = operands
        scores = jnp.dot(query_head, key_head.T, preferred_element_type=jnp.float32) * scale
        scores = jnp.where(valid[None, :], scores, -1e30)
        highest = jnp.max(scores, axis=1, keepdims=True)
        weights = jnp.exp(scores - highest).astype(jnp.bfloat16)
        denominator = jnp.sum(weights.astype(jnp.float32), axis=1, keepdims=True)
        numerator = jnp.dot(weights, value_head, preferred_element_type=jnp.float32)
        return (numerator / denominator).astype(jnp.bfloat16)

    attended = lax.map(one_head, (split_heads(queries, DEC_ROWS), split_heads(memory_keys, ENC_ROWS), split_heads(memory_values, ENC_ROWS)))
    attended = attended.transpose(1, 0, 2).reshape(DEC_ROWS, D)
    projected = lax.dot_general(attended, output_weight, (((1,), (1,)), ((), ())), preferred_element_type=jnp.float32)
    mixed = dec_states.astype(jnp.float32) + projected
    return mixed.astype(jnp.bfloat16)
```

```python
import jax
import jax.numpy as jnp
from jax import lax
from jax.experimental import pallas as pl
from jax.experimental.pallas import tpu as pltpu
from jax.sharding import PartitionSpec as P

MESH = pl.DeviceIdType.MESH
F32, BF16 = jnp.float32, jnp.bfloat16
DH, GROUP = 256, 128
ROWS, FEAT, NZ, NSEQ = 256, 512, 8, 16
HALF, QUART = ROWS // 2, ROWS // 4
BLOCK = 2 * GROUP + 16
NEG = -1e30
DEINT = 32
OFFSETS = (0, -1, 1, -2, 2, -3, 3, 4)
REACH = {("R", 0): 4, ("R", 1): 3, ("L", 1): 4, ("L", 0): 3}
STREAMS = (("R", 0), ("L", 1), ("R", 1), ("L", 0))
NT = (((1,), (1,)), ((), ()))


def slot_of(direction, distance):
    if distance == 0:
        return 0
    if distance == 4:
        return 7
    return 2 * distance - (1 if direction == "R" else 0)


def kernel(enc, dec, weights, lengths, out, xg, stage, w0, w1, wo, acc, kv, kvs, qbuf, qs, dres, att, oacc,
           mx, den, pacc, sbuf, rbuf, load_sem, stage_sem, z_send, z_recv, kv_send, kv_recv, q_send, q_recv,
           wo_send, wo_recv, at_send, at_recv, rs_send, rs_recv):
    s = lax.axis_index("segment")
    q = lax.axis_index("seq")
    m = lax.axis_index("mp")
    y, xh, c = q // 4, (q // 2) % 2, q % 2
    z_to = {"R": (m + 1) % NZ, "L": (m + NZ - 1) % NZ}

    def seq_of(yy, hh, cc):
        return (yy * 2 + hh) * 2 + cc

    y_up, y_down, y_far = (y + 1) % 4, (y + 3) % 4, (y + 2) % 4
    partner = (s, seq_of(y, xh, 1 - c), m)
    up, down = (s, seq_of(y_up, xh, c), m), (s, seq_of(y_down, xh, c), m)
    across = (1 - s, q, m)
    across_other = (1 - s, seq_of(y, 1 - xh, c), m)
    same_other = (s, seq_of(y, 1 - xh, c), m)
    z_dev = {d: (s, q, z_to[d]) for d in ("R", "L")}

    def remote(src, dst, send, recv, device):
        return pltpu.make_async_remote_copy(
            src_ref=src, dst_ref=dst, send_sem=send, recv_sem=recv, device_id=device, device_id_type=MESH
        )

    def load_x(source):
        return pltpu.make_async_copy(source, xg.at[0], load_sem.at[0])

    @pl.when(s == 0)
    def _():
        load_x(enc).start()

    @pl.when(s == 1)
    def _():
        load_x(dec).start()

    load_res = pltpu.make_async_copy(dec, dres, load_sem.at[1])
    load_res.start()

    def shard_of(o):
        return (m + NZ + OFFSETS[o]) % NZ

    def stage_copy(o):
        rows = pl.ds(pl.multiple_of(shard_of(o) * FEAT, FEAT), FEAT)
        return pltpu.make_async_copy(weights.at[0, rows], stage.at[o % 2], stage_sem.at[o % 2])

    stage_copy(0).start()
    stage_copy(1).start()

    barrier = pltpu.get_barrier_semaphore()
    peers = (z_dev["R"], z_dev["L"], up, down, partner, across, across_other, same_other)
    for peer in peers:
        pl.semaphore_signal(barrier, inc=1, device_id=peer, device_id_type=MESH)
    pl.semaphore_wait(barrier, len(peers))

    def z_copy(half, stream, distance):
        direction, sub = stream
        rows = pl.ds(half * HALF + sub * QUART, QUART)
        k = STREAMS.index(stream)
        sems = (half * 4 + k) * 4 + distance - 1
        return remote(
            xg.at[slot_of(direction, distance - 1), rows],
            xg.at[slot_of(direction, distance), rows],
            z_send.at[sems],
            z_recv.at[sems],
            z_dev[direction],
        )

    def z_start(half):
        for stream in STREAMS:
            z_copy(half, stream, 1).start()

    def z_step(half, distance):
        for stream in STREAMS:
            if distance <= REACH[stream]:
                z_copy(half, stream, distance).wait_recv()
                if distance < REACH[stream]:
                    z_copy(half, stream, distance + 1).start()

    def split(o):
        stage_copy(o).wait()
        j = shard_of(o)

        def body(i, carry):
            r = pl.multiple_of(i * DEINT, DEINT)
            pair = jnp.swapaxes(stage[o % 2, pl.ds(r, DEINT)], 0, 1)
            w0[o, pl.ds(r, DEINT), :] = pair[0]
            w1[j, pl.ds(r, DEINT), :] = pair[1]
            return carry

        lax.fori_loop(0, FEAT // DEINT, body, 0, unroll=2)
        if o + 2 < NZ:
            stage_copy(o + 2).start()

    def project(half, o):
        x = xg[o, pl.ds(half * HALF, HALF), :]
        first = jnp.dot(x, w0[o], preferred_element_type=F32)
        if o == 0:
            acc[half, 0] = first
        else:
            acc[half, 0] += first

        @pl.when(s == 0)
        def _():
            second = jnp.dot(x, w1[shard_of(o)], preferred_element_type=F32)
            if o == 0:
                acc[half, 1] = second
            else:
                acc[half, 1] += second

    def kv_index(source, half):
        return half * NSEQ + source

    def kv_copy(src, source, half, which, device):
        return remote(
            src, kv.at[source, half], kv_send.at[half * 20 + which], kv_recv.at[kv_index(source, half)], device
        )

    def kv_wait(source, half):
        kv_copy(kv.at[source, half], source, half, 0, partner).wait_recv()

    def q_copy(half):
        rows = pl.ds(half * HALF, HALF)
        return remote(qs.at[rows], qbuf.at[rows], q_send.at[half], q_recv.at[half], across)

    def x_copies(half):
        return (
            kv_copy(kvs.at[half], q, half, 0, across),
            kv_copy(kvs.at[half], q, half, 1, across_other),
            kv_copy(kv.at[q, half], q, half, 2, same_other),
        )

    def finish(half):
        rows = pl.ds(half * HALF, HALF)

        @pl.when(s == 0)
        def _():
            lane = lax.broadcasted_iota(jnp.int32, (16, DH), 1)
            bias = jnp.where(lane < lengths[half], 0.0, NEG).astype(BF16)
            kvs[half, pl.ds(0, GROUP), :] = acc[half, 0, :, DH:].astype(BF16)
            kvs[half, pl.ds(GROUP, GROUP), :] = acc[half, 1, :, DH:].astype(BF16)
            kvs[half, pl.ds(2 * GROUP, 16), :] = bias
            kv[q, half, pl.ds(0, GROUP), :] = acc[half, 0, :, :DH].astype(BF16)
            kv[q, half, pl.ds(GROUP, GROUP), :] = acc[half, 1, :, :DH].astype(BF16)
            kv[q, half, pl.ds(2 * GROUP, 16), :] = bias
            for copy in x_copies(half):
                copy.start()

        @pl.when(s == 1)
        def _():
            scale = DH ** -0.5
            qs[rows, :] = acc[half, 0, :, :DH].astype(BF16) * jnp.asarray(scale, BF16)
            qbuf[rows, :] = acc[half, 0, :, DH:].astype(BF16) * jnp.asarray(scale, BF16)
            q_copy(half).start()

    def own_sources():
        return [seq_of(y, hh, c) for hh in (0, 1)]

    def y_sends(half):
        near = [(seq_of(y, hh, c), hh) for hh in (0, 1)]
        low = [(seq_of(y_down, hh, c), hh) for hh in (0, 1)]
        high = [(seq_of(y_up, hh, c), hh) for hh in (0, 1)]
        far = [(seq_of(y_far, hh, c), hh) for hh in (0, 1)]
        return near, low, high, far

    def forward(source, half, which, device):
        kv_copy(kv.at[source, half], source, half, which, device).start()

    def y_first(half):
        near, _, _, _ = y_sends(half)
        for source, hh in near:
            @pl.when(jnp.logical_or(s == 1, hh != xh))
            def _():
                kv_wait(source, half)
            forward(source, half, 3 + 2 * hh, up)
            forward(source, half, 4 + 2 * hh, down)
            forward(source, half, 9 + hh, partner)

    def y_second(half):
        _, low, high, _ = y_sends(half)
        (lo0, _), (lo1, _) = low
        (hi0, _), (hi1, _) = high
        kv_wait(lo0, half)
        forward(lo0, half, 7, up)
        forward(lo0, half, 11, partner)
        kv_wait(hi0, half)
        forward(hi0, half, 12, partner)
        kv_wait(hi1, half)
        forward(hi1, half, 8, down)
        forward(hi1, half, 13, partner)
        kv_wait(lo1, half)
        forward(lo1, half, 14, partner)

    def y_third(half):
        _, _, _, far = y_sends(half)
        for source, hh in far:
            kv_wait(source, half)
            forward(source, half, 15 + hh, partner)

    def shared_wait(half):
        for yy in (y, y_down, y_up, y_far):
            for hh in (0, 1):
                kv_wait(seq_of(yy, hh, 1 - c), half)

    TILE = 4

    def attend(half, begin, end):
        queries = qbuf[...]

        def tile(i, carry):
            best, total = carry
            b = i * TILE
            keys = jnp.concatenate([kv[b + j, half, pl.ds(0, GROUP), :] for j in range(TILE)], axis=0)
            values = jnp.concatenate([kv[b + j, half, pl.ds(GROUP, GROUP), :] for j in range(TILE)], axis=0)
            bias = jnp.concatenate(
                [kv[b + j, half, pl.ds(2 * GROUP, 16), pl.ds(0, GROUP)].astype(F32)[0:1] for j in range(TILE)], axis=1
            )
            scores = lax.dot_general(queries, keys, NT, preferred_element_type=F32) + bias
            new_best = jnp.maximum(best, jnp.max(scores, axis=1, keepdims=True))
            shrink = jnp.exp(best - new_best)
            probs = jnp.exp(scores - new_best).astype(BF16)
            total = total * shrink + jnp.sum(probs.astype(F32), axis=1, keepdims=True)
            oacc[...] = oacc[...] * shrink + jnp.dot(probs, values, preferred_element_type=F32)
            return new_best, total

        best, total = lax.fori_loop(begin, end, tile, (mx[:, 0:1], den[:, 0:1]))
        mx[:, 0:1] = best
        den[:, 0:1] = total

    part = xh * 2 + c

    def wo_x_copies():
        return (
            remote(w1.at[part], wo.at[part], wo_send.at[0], wo_recv.at[part], across),
            remote(w1.at[part], wo.at[part], wo_send.at[1], wo_recv.at[part], across_other),
        )

    def wo_share(hh):
        index = hh * 2 + c
        return remote(wo.at[index], wo.at[index], wo_send.at[2 + hh], wo_recv.at[index], partner)

    def wo_wait(index):
        remote(wo.at[index], wo.at[index], wo_send.at[0], wo_recv.at[index], partner).wait_recv()

    def wo_local():
        return pltpu.make_async_copy(w1.at[pl.ds(4, 4)], wo, load_sem.at[2])

    @pl.when(s == 0)
    def _():
        load_x(enc).wait()

    @pl.when(s == 1)
    def _():
        load_x(dec).wait()

    z_start(0)
    mx[...] = jnp.full_like(mx, NEG)
    den[...] = jnp.zeros_like(den)
    oacc[...] = jnp.zeros_like(oacc)
    split(0)
    project(0, 0)
    z_step(0, 1)
    z_start(1)
    split(1)
    project(0, 1)
    split(2)
    project(0, 2)
    z_step(0, 2)
    split(3)
    project(0, 3)
    split(4)
    project(0, 4)
    z_step(0, 3)
    z_step(1, 1)
    split(5)
    project(0, 5)
    split(6)
    project(0, 6)
    z_step(0, 4)
    z_step(1, 2)
    split(7)
    project(0, 7)
    finish(0)

    @pl.when(s == 1)
    def _():
        for copy in wo_x_copies():
            copy.start()
        wo_local().start()

    for o in (0, 1, 2):
        project(1, o)
    y_first(0)
    z_step(1, 3)
    project(1, 3)
    project(1, 4)
    y_second(0)
    z_step(1, 4)
    for o in (5, 6, 7):
        project(1, o)
    finish(1)
    y_third(0)

    @pl.when(s == 0)
    def _():
        q_copy(0).wait_recv()
        q_copy(1).wait_recv()

    y_first(1)
    shared_wait(0)
    attend(0, 0, 2)
    y_second(1)
    attend(0, 2, 4)
    y_third(1)

    @pl.when(s == 0)
    def _():
        for hh in (0, 1):
            wo_wait(hh * 2 + c)
            wo_share(hh).start()

    shared_wait(1)
    attend(1, 0, 4)

    att[s] = (oacc[...] / den[:, 0:1]).astype(BF16)
    att_copy = remote(att.at[s], att.at[s], at_send.at[0], at_recv.at[0], across)
    att_copy.start()

    @pl.when(s == 0)
    def _():
        for hh in (0, 1):
            wo_wait(hh * 2 + 1 - c)

    @pl.when(s == 1)
    def _():
        wo_local().wait()

    load_res.wait()
    remote(att.at[1 - s], att.at[1 - s], at_send.at[0], at_recv.at[0], across).wait_recv()

    def chunk(o):
        d = shard_of(o)
        block = wo[d // 2, pl.ds(pl.multiple_of((d % 2) * DH, DH), DH), :]
        pacc[o] = lax.dot_general(att[0], block[:, :DH], NT, preferred_element_type=F32) + lax.dot_general(
            att[1], block[:, DH:], NT, preferred_element_type=F32
        )

        @pl.when(jnp.logical_and(s == m // 4, d // 2 == m % 4))
        def _():
            columns = pl.ds(pl.multiple_of((d % 2) * DH, DH), DH)
            pacc[o] += dres[:, columns].astype(F32)

    def target(direction, distance):
        if distance == 0:
            return 0
        if distance == 4:
            return 7
        return 2 * distance - (0 if direction == "R" else 1)

    def rs_copy(stream, hop):
        k = STREAMS.index(stream) * 4 + hop
        return remote(sbuf.at[k], rbuf.at[k], rs_send.at[k], rs_recv.at[k], z_dev[stream[0]])

    def rs_start(stream):
        direction, sub = stream
        k = STREAMS.index(stream) * 4
        sbuf[k] = pacc[target(direction, REACH[stream]), pl.ds(sub * HALF, HALF), :].astype(BF16)
        rs_copy(stream, 0).start()

    def rs_step(stream, hop):
        direction, sub = stream
        k = STREAMS.index(stream) * 4 + hop
        rs_copy(stream, hop - 1).wait_recv()
        own = pacc[target(direction, REACH[stream] - hop), pl.ds(sub * HALF, HALF), :]
        sbuf[k] = (own + rbuf[k - 1].astype(F32)).astype(BF16)
        rs_copy(stream, hop).start()

    chunk(7)
    rs_start(("R", 0))
    rs_start(("L", 1))
    chunk(6)
    rs_start(("R", 1))
    chunk(5)
    rs_start(("L", 0))
    for o in (4, 3, 2, 1, 0):
        chunk(o)
    for hop in (1, 2, 3):
        for stream in STREAMS:
            if hop < REACH[stream]:
                rs_step(stream, hop)
    for sub in (0, 1):
        rows = pl.ds(sub * HALF, HALF)
        total = pacc[0, rows, :]
        for direction in ("R", "L"):
            stream = (direction, sub)
            k = STREAMS.index(stream) * 4 + REACH[stream] - 1
            rs_copy(stream, REACH[stream] - 1).wait_recv()
            total = total + rbuf[k].astype(F32)
        out[rows, :] = total.astype(BF16)

    for half in (0, 1):
        for stream in STREAMS:
            for distance in range(1, REACH[stream] + 1):
                z_copy(half, stream, distance).wait_send()
        for which in range(3, 17):
            kv_copy(kv.at[q, half], q, half, which, partner).wait_send()

    @pl.when(s == 0)
    def _():
        for half in (0, 1):
            for copy in x_copies(half):
                copy.wait_send()
        for hh in (0, 1):
            wo_share(hh).wait_send()

    @pl.when(s == 1)
    def _():
        for half in (0, 1):
            q_copy(half).wait_send()
        for copy in wo_x_copies():
            copy.wait_send()

    att_copy.wait_send()
    for stream in STREAMS:
        for hop in range(REACH[stream]):
            rs_copy(stream, hop).wait_send()


def local(enc_states, dec_states, section_weights, group_lengths):
    dma = pltpu.SemaphoreType.DMA
    vmem = pltpu.VMEM
    return pl.pallas_call(
        kernel,
        out_shape=jax.ShapeDtypeStruct((ROWS, DH), BF16),
        in_specs=[pl.BlockSpec(memory_space=pl.ANY)] * 3 + [pl.BlockSpec(memory_space=pltpu.SMEM)],
        out_specs=pl.BlockSpec(memory_space=pltpu.VMEM),
        scratch_shapes=[
            vmem((NZ, ROWS, FEAT), BF16),
            vmem((2, FEAT, 2, FEAT), BF16),
            vmem((NZ, FEAT, FEAT), BF16),
            vmem((NZ, FEAT, FEAT), BF16),
            vmem((4, FEAT, FEAT), BF16),
            vmem((2, 2, HALF, FEAT), F32),
            vmem((NSEQ, 2, BLOCK, DH), BF16),
            vmem((2, BLOCK, DH), BF16),
            vmem((ROWS, DH), BF16),
            vmem((ROWS, DH), BF16),
            vmem((ROWS, FEAT), BF16),
            vmem((2, ROWS, DH), BF16),
            vmem((ROWS, DH), F32),
            vmem((ROWS, 128), F32),
            vmem((ROWS, 128), F32),
            vmem((NZ, ROWS, DH), F32),
            vmem((16, HALF, DH), BF16),
            vmem((16, HALF, DH), BF16),
            dma((3,)),
            dma((2,)),
            dma((32,)),
            dma((32,)),
            dma((40,)),
            dma((32,)),
            dma((2,)),
            dma((2,)),
            dma((4,)),
            dma((4,)),
            dma((1,)),
            dma((1,)),
            dma((16,)),
            dma((16,)),
        ],
        compiler_params=pltpu.CompilerParams(
            collective_id=0, has_side_effects=True, vmem_limit_bytes=60 * 2**20
        ),
    )(enc_states, dec_states, section_weights, group_lengths)


def solution(mesh):
    in_specs = (P("seq", "mp"), P("seq", "mp"), P("segment", None, None, "mp"), P("seq"))
    out_specs = P("seq", ("segment", "mp"))
    return jax.shard_map(local, mesh=mesh, in_specs=in_specs, out_specs=out_specs, check_vma=False)
```

```python
import jax
import jax.numpy as jnp
from jax import lax
from jax.experimental import pallas as pl
from jax.experimental.pallas import tpu as pltpu
from jax.sharding import PartitionSpec as P

MESH = pl.DeviceIdType.MESH
F32, BF16 = jnp.float32, jnp.bfloat16
DH, GROUP = 256, 128
ROWS, FEAT, NZ, NSEQ = 256, 512, 8, 16
HALF, QUART = ROWS // 2, ROWS // 4
VROWS = GROUP + 16
NEG = -1e30
DEINT = 32
OFFSETS = (0, -1, 1, -2, 2, -3, 3, 4)
REACH = {("R", 0): 4, ("R", 1): 3, ("L", 1): 4, ("L", 0): 3}
STREAMS = (("R", 0), ("L", 1), ("R", 1), ("L", 0))
NT = (((1,), (1,)), ((), ()))


def slot_of(direction, distance):
    if distance == 0:
        return 0
    if distance == 4:
        return 7
    return 2 * distance - (1 if direction == "R" else 0)


def kernel(enc, dec, weights, lengths, out, xg, stage, w0, w1, wo, acc, kb, vb, ks, vs, qbuf, qs, dres, att, oacc,
           mx, den, pacc, sbuf, rbuf, load_sem, stage_sem, z_send, z_recv, kv_send, kv_recv, q_send, q_recv,
           wo_send, wo_recv, at_send, at_recv, rs_send, rs_recv):
    s = lax.axis_index("segment")
    q = lax.axis_index("seq")
    m = lax.axis_index("mp")
    y, xh, c = q // 4, (q // 2) % 2, q % 2
    z_to = {"R": (m + 1) % NZ, "L": (m + NZ - 1) % NZ}

    def seq_of(yy, hh, cc):
        return (yy * 2 + hh) * 2 + cc

    y_up, y_down, y_far = (y + 1) % 4, (y + 3) % 4, (y + 2) % 4
    partner = (s, seq_of(y, xh, 1 - c), m)
    up, down = (s, seq_of(y_up, xh, c), m), (s, seq_of(y_down, xh, c), m)
    across = (1 - s, q, m)
    across_other = (1 - s, seq_of(y, 1 - xh, c), m)
    same_other = (s, seq_of(y, 1 - xh, c), m)
    z_dev = {d: (s, q, z_to[d]) for d in ("R", "L")}

    def remote(src, dst, send, recv, device):
        return pltpu.make_async_remote_copy(
            src_ref=src, dst_ref=dst, send_sem=send, recv_sem=recv, device_id=device, device_id_type=MESH
        )

    def load_x(source):
        return pltpu.make_async_copy(source, xg.at[0], load_sem.at[0])

    @pl.when(s == 0)
    def _():
        load_x(enc).start()

    @pl.when(s == 1)
    def _():
        load_x(dec).start()

    load_res = pltpu.make_async_copy(dec, dres, load_sem.at[1])
    load_res.start()

    def shard_of(o):
        return (m + NZ + OFFSETS[o]) % NZ

    def stage_copy(o):
        rows = pl.ds(pl.multiple_of(shard_of(o) * FEAT, FEAT), FEAT)
        return pltpu.make_async_copy(weights.at[0, rows], stage.at[o % 2], stage_sem.at[o % 2])

    stage_copy(0).start()
    stage_copy(1).start()

    barrier = pltpu.get_barrier_semaphore()
    peers = (z_dev["R"], z_dev["L"], up, down, partner, across, across_other, same_other)
    for peer in peers:
        pl.semaphore_signal(barrier, inc=1, device_id=peer, device_id_type=MESH)
    pl.semaphore_wait(barrier, len(peers))

    def z_copy(half, stream, distance):
        direction, sub = stream
        rows = pl.ds(half * HALF + sub * QUART, QUART)
        k = STREAMS.index(stream)
        sems = (half * 4 + k) * 4 + distance - 1
        return remote(
            xg.at[slot_of(direction, distance - 1), rows],
            xg.at[slot_of(direction, distance), rows],
            z_send.at[sems],
            z_recv.at[sems],
            z_dev[direction],
        )

    def z_start(half):
        for stream in STREAMS:
            z_copy(half, stream, 1).start()

    def z_step(half, distance):
        for stream in STREAMS:
            if distance <= REACH[stream]:
                z_copy(half, stream, distance).wait_recv()
                if distance < REACH[stream]:
                    z_copy(half, stream, distance + 1).start()

    def split(o):
        stage_copy(o).wait()
        j = shard_of(o)

        def body(i, carry):
            r = pl.multiple_of(i * DEINT, DEINT)
            pair = jnp.swapaxes(stage[o % 2, pl.ds(r, DEINT)], 0, 1)
            w0[o, pl.ds(r, DEINT), :] = pair[0]
            w1[j, pl.ds(r, DEINT), :] = pair[1]
            return carry

        lax.fori_loop(0, FEAT // DEINT, body, 0, unroll=2)
        if o + 2 < NZ:
            stage_copy(o + 2).start()

    def project(half, o):
        x = xg[o, pl.ds(half * HALF, HALF), :]
        first = jnp.dot(x, w0[o], preferred_element_type=F32)
        if o == 0:
            acc[half, 0] = first
        else:
            acc[half, 0] += first

        @pl.when(s == 0)
        def _():
            second = jnp.dot(x, w1[shard_of(o)], preferred_element_type=F32)
            if o == 0:
                acc[half, 1] = second
            else:
                acc[half, 1] += second

    def piece(source, half, p):
        return kb.at[source, half] if p == 0 else vb.at[source, half]

    def kv_copy(src, source, half, p, which, device):
        return remote(
            src,
            piece(source, half, p),
            kv_send.at[(half * 2 + p) * 17 + which],
            kv_recv.at[(half * 2 + p) * NSEQ + source],
            device,
        )

    def kv_wait(source, half, p):
        kv_copy(piece(source, half, p), source, half, p, 0, partner).wait_recv()

    def forward(source, half, p, which, device):
        kv_copy(piece(source, half, p), source, half, p, which, device).start()

    def q_copy(half):
        rows = pl.ds(half * HALF, HALF)
        return remote(qs.at[rows], qbuf.at[rows], q_send.at[half], q_recv.at[half], across)

    def x_copies(half, p):
        other = ks.at[half] if p == 0 else vs.at[half]
        return (
            kv_copy(other, q, half, p, 0, across),
            kv_copy(other, q, half, p, 1, across_other),
            kv_copy(piece(q, half, p), q, half, p, 2, same_other),
        )

    def finish(half):
        rows = pl.ds(half * HALF, HALF)

        @pl.when(s == 0)
        def _():
            ks[half] = acc[half, 0, :, DH:].astype(BF16)
            kb[q, half] = acc[half, 0, :, :DH].astype(BF16)
            for copy in x_copies(half, 0):
                copy.start()
            lane = lax.broadcasted_iota(jnp.int32, (16, DH), 1)
            bias = jnp.where(lane < lengths[half], 0.0, NEG).astype(BF16)
            vs[half, pl.ds(0, GROUP), :] = acc[half, 1, :, DH:].astype(BF16)
            vs[half, pl.ds(GROUP, 16), :] = bias
            vb[q, half, pl.ds(0, GROUP), :] = acc[half, 1, :, :DH].astype(BF16)
            vb[q, half, pl.ds(GROUP, 16), :] = bias
            for copy in x_copies(half, 1):
                copy.start()

        @pl.when(s == 1)
        def _():
            scale = DH ** -0.5
            qs[rows, :] = acc[half, 0, :, :DH].astype(BF16) * jnp.asarray(scale, BF16)
            qbuf[rows, :] = acc[half, 0, :, DH:].astype(BF16) * jnp.asarray(scale, BF16)
            q_copy(half).start()

    def source_of(yy, k):
        return seq_of(yy, xh if k == 0 else 1 - xh, c)

    def y_near(half, k, local_source):
        source = source_of(y, k)
        for p in (0, 1):
            if not local_source:
                kv_wait(source, half, p)
            forward(source, half, p, 3 + 2 * k, up)
            forward(source, half, p, 4 + 2 * k, down)
            forward(source, half, p, 8 + k, partner)

    def y_next(half, k):
        low, high = source_of(y_down, k), source_of(y_up, k)
        kv_wait(low, half, 0)
        forward(low, half, 0, 7 if k == 0 else 10, up)
        forward(low, half, 0, 11 + k, partner)
        kv_wait(high, half, 0)
        forward(high, half, 0, 13 + k, partner)
        kv_wait(high, half, 1)
        forward(high, half, 1, 7 if k == 0 else 10, down)
        forward(high, half, 1, 13 + k, partner)
        kv_wait(low, half, 1)
        forward(low, half, 1, 11 + k, partner)

    def y_far_in(half, k):
        source = source_of(y_far, k)
        for p in (0, 1):
            kv_wait(source, half, p)
            forward(source, half, p, 15 + k, partner)

    def shared_wait(half, yy):
        for hh in (0, 1):
            for p in (0, 1):
                kv_wait(seq_of(yy, hh, 1 - c), half, p)

    def attend(half, yy):
        b = yy * 4
        keys = jnp.concatenate([kb[b + j, half] for j in range(4)], axis=0)
        values = jnp.concatenate([vb[b + j, half, pl.ds(0, GROUP), :] for j in range(4)], axis=0)
        bias = jnp.concatenate(
            [vb[b + j, half, pl.ds(GROUP, 16), pl.ds(0, GROUP)].astype(F32)[0:1] for j in range(4)], axis=1
        )
        best, total = mx[:, 0:1], den[:, 0:1]
        scores = lax.dot_general(qbuf[...], keys, NT, preferred_element_type=F32) + bias
        new_best = jnp.maximum(best, jnp.max(scores, axis=1, keepdims=True))
        shrink = jnp.exp(best - new_best)
        probs = jnp.exp(scores - new_best).astype(BF16)
        mx[:, 0:1] = new_best
        den[:, 0:1] = total * shrink + jnp.sum(probs.astype(F32), axis=1, keepdims=True)
        oacc[...] = oacc[...] * shrink + jnp.dot(probs, values, preferred_element_type=F32)

    part = xh * 2 + c

    def wo_x_copies():
        return (
            remote(w1.at[part], wo.at[part], wo_send.at[0], wo_recv.at[part], across),
            remote(w1.at[part], wo.at[part], wo_send.at[1], wo_recv.at[part], across_other),
        )

    def wo_share(hh):
        index = hh * 2 + c
        return remote(wo.at[index], wo.at[index], wo_send.at[2 + hh], wo_recv.at[index], partner)

    def wo_wait(index):
        remote(wo.at[index], wo.at[index], wo_send.at[0], wo_recv.at[index], partner).wait_recv()

    def wo_local():
        return pltpu.make_async_copy(w1.at[pl.ds(4, 4)], wo, load_sem.at[2])

    @pl.when(s == 0)
    def _():
        load_x(enc).wait()

    @pl.when(s == 1)
    def _():
        load_x(dec).wait()

    def enc_side(body, *args):
        @pl.when(s == 0)
        def _():
            body(*args)

    def dec_side(body, *args):
        @pl.when(s == 1)
        def _():
            body(*args)

    z_start(0)
    mx[...] = jnp.full_like(mx, NEG)
    den[...] = jnp.zeros_like(den)
    oacc[...] = jnp.zeros_like(oacc)
    split(0)
    project(0, 0)
    z_step(0, 1)
    z_start(1)
    split(1)
    project(0, 1)
    split(2)
    project(0, 2)
    z_step(0, 2)
    z_step(1, 1)
    split(3)
    project(0, 3)
    split(4)
    project(0, 4)
    z_step(0, 3)
    z_step(1, 2)
    split(5)
    project(0, 5)
    split(6)
    project(0, 6)
    split(7)
    z_step(0, 4)
    project(0, 7)
    finish(0)
    enc_side(y_near, 0, 0, True)

    @pl.when(s == 1)
    def _():
        for copy in wo_x_copies():
            copy.start()
        wo_local().start()

    z_step(1, 3)
    for o in (0, 1, 2, 3, 4):
        project(1, o)
    dec_side(y_near, 0, 0, False)
    dec_side(y_near, 0, 1, False)
    y_next(0, 0)
    for o in (5, 6):
        project(1, o)
    z_step(1, 4)
    project(1, 7)
    finish(1)
    enc_side(y_near, 1, 0, True)
    enc_side(y_near, 0, 1, False)
    y_next(0, 1)
    y_far_in(0, 0)
    y_far_in(0, 1)

    @pl.when(s == 0)
    def _():
        q_copy(0).wait_recv()
        q_copy(1).wait_recv()

    dec_side(y_near, 1, 0, False)
    dec_side(y_near, 1, 1, False)
    y_next(1, 0)
    shared_wait(0, y)
    attend(0, y)
    enc_side(y_near, 1, 1, False)
    shared_wait(0, y_down)
    attend(0, y_down)
    y_next(1, 1)
    shared_wait(0, y_up)
    attend(0, y_up)
    shared_wait(0, y_far)
    attend(0, y_far)
    y_far_in(1, 0)

    @pl.when(s == 0)
    def _():
        for hh in (0, 1):
            wo_wait(hh * 2 + c)
            wo_share(hh).start()

    shared_wait(1, y)
    attend(1, y)
    y_far_in(1, 1)
    shared_wait(1, y_down)
    attend(1, y_down)
    shared_wait(1, y_up)
    attend(1, y_up)
    shared_wait(1, y_far)
    attend(1, y_far)

    att[s] = (oacc[...] / den[:, 0:1]).astype(BF16)
    att_copy = remote(att.at[s], att.at[s], at_send.at[0], at_recv.at[0], across)
    att_copy.start()

    @pl.when(s == 0)
    def _():
        for hh in (0, 1):
            wo_wait(hh * 2 + 1 - c)

    @pl.when(s == 1)
    def _():
        wo_local().wait()

    load_res.wait()
    remote(att.at[1 - s], att.at[1 - s], at_send.at[0], at_recv.at[0], across).wait_recv()

    def chunk(o):
        d = shard_of(o)
        block = wo[d // 2, pl.ds(pl.multiple_of((d % 2) * DH, DH), DH), :]
        pacc[o] = lax.dot_general(att[0], block[:, :DH], NT, preferred_element_type=F32) + lax.dot_general(
            att[1], block[:, DH:], NT, preferred_element_type=F32
        )

        @pl.when(jnp.logical_and(s == m // 4, d // 2 == m % 4))
        def _():
            columns = pl.ds(pl.multiple_of((d % 2) * DH, DH), DH)
            pacc[o] += dres[:, columns].astype(F32)

    def target(direction, distance):
        if distance == 0:
            return 0
        if distance == 4:
            return 7
        return 2 * distance - (0 if direction == "R" else 1)

    def rs_copy(stream, hop):
        k = STREAMS.index(stream) * 4 + hop
        return remote(sbuf.at[k], rbuf.at[k], rs_send.at[k], rs_recv.at[k], z_dev[stream[0]])

    def rs_start(stream):
        direction, sub = stream
        k = STREAMS.index(stream) * 4
        sbuf[k] = pacc[target(direction, REACH[stream]), pl.ds(sub * HALF, HALF), :].astype(BF16)
        rs_copy(stream, 0).start()

    def rs_step(stream, hop):
        direction, sub = stream
        k = STREAMS.index(stream) * 4 + hop
        rs_copy(stream, hop - 1).wait_recv()
        own = pacc[target(direction, REACH[stream] - hop), pl.ds(sub * HALF, HALF), :]
        sbuf[k] = (own + rbuf[k - 1].astype(F32)).astype(BF16)
        rs_copy(stream, hop).start()

    chunk(7)
    rs_start(("R", 0))
    rs_start(("L", 1))
    chunk(6)
    rs_start(("R", 1))
    chunk(5)
    rs_start(("L", 0))
    for o in (4, 3, 2, 1, 0):
        chunk(o)
    for hop in (1, 2, 3):
        for stream in STREAMS:
            if hop < REACH[stream]:
                rs_step(stream, hop)
    for sub in (0, 1):
        rows = pl.ds(sub * HALF, HALF)
        total = pacc[0, rows, :]
        for direction in ("R", "L"):
            stream = (direction, sub)
            k = STREAMS.index(stream) * 4 + REACH[stream] - 1
            rs_copy(stream, REACH[stream] - 1).wait_recv()
            total = total + rbuf[k].astype(F32)
        out[rows, :] = total.astype(BF16)

    for half in (0, 1):
        for stream in STREAMS:
            for distance in range(1, REACH[stream] + 1):
                z_copy(half, stream, distance).wait_send()
        for p in (0, 1):
            for which in range(3, 17):
                kv_copy(piece(q, half, p), q, half, p, which, partner).wait_send()

    @pl.when(s == 0)
    def _():
        for half in (0, 1):
            for p in (0, 1):
                for copy in x_copies(half, p):
                    copy.wait_send()
        for hh in (0, 1):
            wo_share(hh).wait_send()

    @pl.when(s == 1)
    def _():
        for half in (0, 1):
            q_copy(half).wait_send()
        for copy in wo_x_copies():
            copy.wait_send()

    att_copy.wait_send()
    for stream in STREAMS:
        for hop in range(REACH[stream]):
            rs_copy(stream, hop).wait_send()


def local(enc_states, dec_states, section_weights, group_lengths):
    dma = pltpu.SemaphoreType.DMA
    vmem = pltpu.VMEM
    return pl.pallas_call(
        kernel,
        out_shape=jax.ShapeDtypeStruct((ROWS, DH), BF16),
        in_specs=[pl.BlockSpec(memory_space=pl.ANY)] * 3 + [pl.BlockSpec(memory_space=pltpu.SMEM)],
        out_specs=pl.BlockSpec(memory_space=pltpu.VMEM),
        scratch_shapes=[
            vmem((NZ, ROWS, FEAT), BF16),
            vmem((2, FEAT, 2, FEAT), BF16),
            vmem((NZ, FEAT, FEAT), BF16),
            vmem((NZ, FEAT, FEAT), BF16),
            vmem((4, FEAT, FEAT), BF16),
            vmem((2, 2, HALF, FEAT), F32),
            vmem((NSEQ, 2, GROUP, DH), BF16),
            vmem((NSEQ, 2, VROWS, DH), BF16),
            vmem((2, GROUP, DH), BF16),
            vmem((2, VROWS, DH), BF16),
            vmem((ROWS, DH), BF16),
            vmem((ROWS, DH), BF16),
            vmem((ROWS, FEAT), BF16),
            vmem((2, ROWS, DH), BF16),
            vmem((ROWS, DH), F32),
            vmem((ROWS, 128), F32),
            vmem((ROWS, 128), F32),
            vmem((NZ, ROWS, DH), F32),
            vmem((16, HALF, DH), BF16),
            vmem((16, HALF, DH), BF16),
            dma((3,)),
            dma((2,)),
            dma((32,)),
            dma((32,)),
            dma((68,)),
            dma((64,)),
            dma((2,)),
            dma((2,)),
            dma((4,)),
            dma((4,)),
            dma((1,)),
            dma((1,)),
            dma((16,)),
            dma((16,)),
        ],
        compiler_params=pltpu.CompilerParams(
            collective_id=0, has_side_effects=True, vmem_limit_bytes=60 * 2**20
        ),
    )(enc_states, dec_states, section_weights, group_lengths)


def solution(mesh):
    in_specs = (P("seq", "mp"), P("seq", "mp"), P("segment", None, None, "mp"), P("seq"))
    out_specs = P("seq", ("segment", "mp"))
    return jax.shard_map(local, mesh=mesh, in_specs=in_specs, out_specs=out_specs, check_vma=False)
```

```python
import jax
import jax.numpy as jnp
from jax import lax
from jax.experimental import pallas as pl
from jax.experimental.pallas import tpu as pltpu
from jax.sharding import PartitionSpec as P

MESH = pl.DeviceIdType.MESH
F32, BF16 = jnp.float32, jnp.bfloat16
DH, GROUP = 256, 128
ROWS, FEAT, NZ, NSEQ = 256, 512, 8, 16
HALF, QUART = ROWS // 2, ROWS // 4
VROWS = GROUP + 16
NEG = -1e30
DEINT = 32
OFFSETS = (0, -1, 1, -2, 2, -3, 3, 4)
REACH = {("R", 0): 4, ("R", 1): 3, ("L", 1): 4, ("L", 0): 3}
STREAMS = (("R", 0), ("L", 1), ("R", 1), ("L", 0))
NT = (((1,), (1,)), ((), ()))


def slot_of(direction, distance):
    if distance == 0:
        return 0
    if distance == 4:
        return 7
    return 2 * distance - (1 if direction == "R" else 0)


def kernel(enc, dec, weights, lengths, out, xg, stage, w0, w1, wo, acc, kb, vb, ks, vs, qbuf, qs, dres, att, oacc,
           mx, den, ps, psm, pr, prm, pacc, sbuf, rbuf, load_sem, stage_sem, z_send, z_recv, kv_send, kv_recv, q_send, q_recv,
           wo_send, wo_recv, p_send, p_recv, rs_send, rs_recv):
    s = lax.axis_index("segment")
    q = lax.axis_index("seq")
    m = lax.axis_index("mp")
    y, xh, c = q // 4, (q // 2) % 2, q % 2
    z_to = {"R": (m + 1) % NZ, "L": (m + NZ - 1) % NZ}

    def seq_of(yy, hh, cc):
        return (yy * 2 + hh) * 2 + cc

    y_up, y_down, y_far = (y + 1) % 4, (y + 3) % 4, (y + 2) % 4
    partner = (s, seq_of(y, xh, 1 - c), m)
    up, down = (s, seq_of(y_up, xh, c), m), (s, seq_of(y_down, xh, c), m)
    across = (1 - s, q, m)
    across_other = (1 - s, seq_of(y, 1 - xh, c), m)
    same_other = (s, seq_of(y, 1 - xh, c), m)
    z_dev = {d: (s, q, z_to[d]) for d in ("R", "L")}

    def remote(src, dst, send, recv, device):
        return pltpu.make_async_remote_copy(
            src_ref=src, dst_ref=dst, send_sem=send, recv_sem=recv, device_id=device, device_id_type=MESH
        )

    def load_x(source):
        return pltpu.make_async_copy(source, xg.at[0], load_sem.at[0])

    @pl.when(s == 0)
    def _():
        load_x(enc).start()

    @pl.when(s == 1)
    def _():
        load_x(dec).start()

    load_res = pltpu.make_async_copy(dec, dres, load_sem.at[1])
    load_res.start()

    def shard_of(o):
        return (m + NZ + OFFSETS[o]) % NZ

    def stage_copy(o):
        rows = pl.ds(pl.multiple_of(shard_of(o) * FEAT, FEAT), FEAT)
        return pltpu.make_async_copy(weights.at[0, rows], stage.at[o % 2], stage_sem.at[o % 2])

    stage_copy(0).start()
    stage_copy(1).start()

    barrier = pltpu.get_barrier_semaphore()
    peers = (z_dev["R"], z_dev["L"], up, down, partner, across, across_other, same_other)
    for peer in peers:
        pl.semaphore_signal(barrier, inc=1, device_id=peer, device_id_type=MESH)
    pl.semaphore_wait(barrier, len(peers))

    def z_copy(half, stream, distance):
        direction, sub = stream
        rows = pl.ds(half * HALF + sub * QUART, QUART)
        k = STREAMS.index(stream)
        sems = (half * 4 + k) * 4 + distance - 1
        return remote(
            xg.at[slot_of(direction, distance - 1), rows],
            xg.at[slot_of(direction, distance), rows],
            z_send.at[sems],
            z_recv.at[sems],
            z_dev[direction],
        )

    def z_start(half):
        for stream in STREAMS:
            z_copy(half, stream, 1).start()

    def z_step(half, distance):
        for stream in STREAMS:
            if distance <= REACH[stream]:
                z_copy(half, stream, distance).wait_recv()
                if distance < REACH[stream]:
                    z_copy(half, stream, distance + 1).start()

    def split(o):
        stage_copy(o).wait()
        j = shard_of(o)

        def body(i, carry):
            r = pl.multiple_of(i * DEINT, DEINT)
            pair = jnp.swapaxes(stage[o % 2, pl.ds(r, DEINT)], 0, 1)
            w0[o, pl.ds(r, DEINT), :] = pair[0]
            w1[j, pl.ds(r, DEINT), :] = pair[1]
            return carry

        lax.fori_loop(0, FEAT // DEINT, body, 0, unroll=2)
        if o + 2 < NZ:
            stage_copy(o + 2).start()

    def project(half, o):
        x = xg[o, pl.ds(half * HALF, HALF), :]
        first = jnp.dot(x, w0[o], preferred_element_type=F32)
        if o == 0:
            acc[half, 0] = first
        else:
            acc[half, 0] += first

        @pl.when(s == 0)
        def _():
            second = jnp.dot(x, w1[shard_of(o)], preferred_element_type=F32)
            if o == 0:
                acc[half, 1] = second
            else:
                acc[half, 1] += second

    def piece(index, half, p):
        return kb.at[index, half] if p == 0 else vb.at[index, half]

    def kv_copy(src, index, half, p, which, device):
        return remote(
            src,
            piece(index, half, p),
            kv_send.at[(half * 2 + p) * 8 + which],
            kv_recv.at[(half * 2 + p) * 8 + index],
            device,
        )

    def kv_wait(index, half, p):
        kv_copy(piece(index, half, p), index, half, p, 0, partner).wait_recv()

    def forward(index, half, p, which, device):
        kv_copy(piece(index, half, p), index, half, p, which, device).start()

    def x_copy(half, p):
        return kv_copy(ks.at[half] if p == 0 else vs.at[half], y * 2 + c, half, p, 0, across)

    def q_copies(half):
        rows = pl.ds(half * HALF, HALF)
        return (
            remote(qs.at[rows], qbuf.at[0, rows], q_send.at[half * 3], q_recv.at[half * 2], across),
            remote(qs.at[rows], qbuf.at[1, rows], q_send.at[half * 3 + 1], q_recv.at[half * 2 + 1], across_other),
            remote(qbuf.at[0, rows], qbuf.at[1, rows], q_send.at[half * 3 + 2], q_recv.at[half * 2 + 1], same_other),
        )

    def finish(half):
        rows = pl.ds(half * HALF, HALF)
        own = y * 2 + c

        @pl.when(s == 0)
        def _():
            ks[half] = acc[half, 0, :, DH:].astype(BF16)
            x_copy(half, 0).start()
            kb[own, half] = acc[half, 0, :, :DH].astype(BF16)
            lane = lax.broadcasted_iota(jnp.int32, (16, DH), 1)
            bias = jnp.where(lane < lengths[half], 0.0, NEG).astype(BF16)
            vs[half, pl.ds(0, GROUP), :] = acc[half, 1, :, DH:].astype(BF16)
            vs[half, pl.ds(GROUP, 16), :] = bias
            x_copy(half, 1).start()
            vb[own, half, pl.ds(0, GROUP), :] = acc[half, 1, :, :DH].astype(BF16)
            vb[own, half, pl.ds(GROUP, 16), :] = bias

        @pl.when(s == 1)
        def _():
            scale = DH ** -0.5
            qs[rows, :] = acc[half, 0, :, :DH].astype(BF16) * jnp.asarray(scale, BF16)
            qbuf[0, rows, :] = acc[half, 0, :, DH:].astype(BF16) * jnp.asarray(scale, BF16)
            for copy in q_copies(half):
                copy.start()

    def y_near(half, local_source):
        for p in (0, 1):
            if not local_source:
                kv_wait(y * 2 + c, half, p)
            forward(y * 2 + c, half, p, 1, up)
            forward(y * 2 + c, half, p, 2, down)
            forward(y * 2 + c, half, p, 3, partner)

    def y_next(half):
        low, high = y_down * 2 + c, y_up * 2 + c
        kv_wait(low, half, 0)
        forward(low, half, 0, 4, up)
        forward(low, half, 0, 5, partner)
        kv_wait(high, half, 0)
        forward(high, half, 0, 6, partner)
        kv_wait(high, half, 1)
        forward(high, half, 1, 4, down)
        forward(high, half, 1, 6, partner)
        kv_wait(low, half, 1)
        forward(low, half, 1, 5, partner)

    def y_last(half):
        for p in (0, 1):
            kv_wait(y_far * 2 + c, half, p)
            forward(y_far * 2 + c, half, p, 7, partner)

    def shared_wait(half, *positions):
        for yy in positions:
            for p in (0, 1):
                kv_wait(yy * 2 + 1 - c, half, p)

    def attend(half, first, second, k):
        blocks = (first * 2, first * 2 + 1, second * 2, second * 2 + 1)
        keys = jnp.concatenate([kb[b, half] for b in blocks], axis=0)
        values = jnp.concatenate([vb[b, half, pl.ds(0, GROUP), :] for b in blocks], axis=0)
        bias = jnp.concatenate(
            [vb[b, half, pl.ds(GROUP, 16), pl.ds(0, GROUP)].astype(F32)[0:1] for b in blocks], axis=1
        )
        best, total = mx[k, :, 0:1], den[k, :, 0:1]
        scores = lax.dot_general(qbuf[k], keys, NT, preferred_element_type=F32) + bias
        new_best = jnp.maximum(best, jnp.max(scores, axis=1, keepdims=True))
        shrink = jnp.exp(best - new_best)
        probs = jnp.exp(scores - new_best).astype(BF16)
        mx[k] = jnp.broadcast_to(new_best, (ROWS, 128))
        den[k] = jnp.broadcast_to(total * shrink + jnp.sum(probs.astype(F32), axis=1, keepdims=True), (ROWS, 128))
        oacc[k] = oacc[k] * shrink + jnp.dot(probs, values, preferred_element_type=F32)

    def part_copies(k, device):
        return (
            remote(ps.at[k], pr.at[k], p_send.at[2 * k], p_recv.at[2 * k], device),
            remote(psm.at[k], prm.at[k], p_send.at[2 * k + 1], p_recv.at[2 * k + 1], device),
        )

    def part_send(k):
        ps[k] = oacc[k].astype(BF16)
        psm[k, pl.ds(0, 8), :] = jnp.transpose(mx[k])[0:8]
        psm[k, pl.ds(8, 8), :] = jnp.transpose(den[k])[0:8]
        for copy in part_copies(k, across if k == 0 else across_other):
            copy.start()

    def relay_copies():
        return (
            remote(pr.at[1], pr.at[2], p_send.at[4], p_recv.at[4], across),
            remote(prm.at[1], prm.at[2], p_send.at[5], p_recv.at[5], across),
        )

    def column(row):
        return jnp.transpose(jnp.broadcast_to(row, (128, ROWS)))[:, 0:1]

    def merge(head, one, one_best, one_sum, two, two_best, two_sum):
        best = jnp.maximum(one_best, two_best)
        one_share, two_share = jnp.exp(one_best - best), jnp.exp(two_best - best)
        scale = 1.0 / (one_sum * one_share + two_sum * two_share)
        att[head] = (one * (one_share * scale) + two * (two_share * scale)).astype(BF16)

    def received(slot):
        return pr[slot].astype(F32), column(prm[slot, 0:1, :]), column(prm[slot, 8:9, :])

    part = xh * 2 + c

    def wo_x_copies():
        return (
            remote(w1.at[part], wo.at[part], wo_send.at[0], wo_recv.at[part], across),
            remote(w1.at[part], wo.at[part], wo_send.at[1], wo_recv.at[part], across_other),
        )

    def wo_share(hh):
        index = hh * 2 + c
        return remote(wo.at[index], wo.at[index], wo_send.at[2 + hh], wo_recv.at[index], partner)

    def wo_wait(index):
        remote(wo.at[index], wo.at[index], wo_send.at[0], wo_recv.at[index], partner).wait_recv()

    def wo_local():
        return pltpu.make_async_copy(w1.at[pl.ds(4, 4)], wo, load_sem.at[2])

    @pl.when(s == 0)
    def _():
        load_x(enc).wait()

    @pl.when(s == 1)
    def _():
        load_x(dec).wait()

    def enc_side(body, *args):
        @pl.when(s == 0)
        def _():
            body(*args)

    def dec_side(body, *args):
        @pl.when(s == 1)
        def _():
            body(*args)

    z_start(0)
    mx[...] = jnp.full_like(mx, NEG)
    den[...] = jnp.zeros_like(den)
    oacc[...] = jnp.zeros_like(oacc)
    split(0)
    project(0, 0)
    z_step(0, 1)
    z_start(1)
    split(1)
    project(0, 1)
    split(2)
    project(0, 2)
    z_step(0, 2)
    z_step(1, 1)
    split(3)
    project(0, 3)
    split(4)
    project(0, 4)
    z_step(0, 3)
    z_step(1, 2)
    split(5)
    project(0, 5)
    split(6)
    project(0, 6)
    split(7)
    z_step(0, 4)
    project(0, 7)
    finish(0)
    enc_side(y_near, 0, True)

    @pl.when(s == 1)
    def _():
        for copy in wo_x_copies():
            copy.start()
        wo_local().start()

    z_step(1, 3)
    for o in (0, 1, 2, 3, 4):
        project(1, o)
    dec_side(y_near, 0, False)
    y_next(0)
    for o in (5, 6):
        project(1, o)
    z_step(1, 4)
    project(1, 7)
    finish(1)
    enc_side(y_near, 1, True)
    y_last(0)
    for half in (0, 1):
        q_copies(half)[1].wait_recv()

    @pl.when(s == 0)
    def _():
        for half in (0, 1):
            q_copies(half)[0].wait_recv()

    shared_wait(0, y, y_down)
    attend(0, y, y_down, 1)
    attend(0, y, y_down, 0)
    dec_side(y_near, 1, False)
    shared_wait(0, y_up, y_far)
    attend(0, y_up, y_far, 1)
    attend(0, y_up, y_far, 0)
    y_next(1)

    @pl.when(s == 0)
    def _():
        for hh in (0, 1):
            wo_wait(hh * 2 + c)
            wo_share(hh).start()

    y_last(1)
    shared_wait(1, y, y_down)
    attend(1, y, y_down, 1)
    attend(1, y, y_down, 0)
    shared_wait(1, y_up, y_far)
    attend(1, y_up, y_far, 1)
    part_send(1)
    attend(1, y_up, y_far, 0)
    part_send(0)

    @pl.when(s == 0)
    def _():
        for hh in (0, 1):
            wo_wait(hh * 2 + 1 - c)

    @pl.when(s == 1)
    def _():
        wo_local().wait()

    load_res.wait()
    for copy in part_copies(1, across_other):
        copy.wait_recv()
    for copy in relay_copies():
        copy.start()
    for copy in part_copies(0, across):
        copy.wait_recv()
    merge(1 - s, *received(0), *received(1))
    for copy in relay_copies():
        copy.wait_recv()
    merge(s, oacc[0], mx[0, :, 0:1], den[0, :, 0:1], *received(2))

    def chunk(o):
        d = shard_of(o)
        block = wo[d // 2, pl.ds(pl.multiple_of((d % 2) * DH, DH), DH), :]
        pacc[o] = lax.dot_general(att[0], block[:, :DH], NT, preferred_element_type=F32) + lax.dot_general(
            att[1], block[:, DH:], NT, preferred_element_type=F32
        )

        @pl.when(jnp.logical_and(s == m // 4, d // 2 == m % 4))
        def _():
            columns = pl.ds(pl.multiple_of((d % 2) * DH, DH), DH)
            pacc[o] += dres[:, columns].astype(F32)

    def target(direction, distance):
        if distance == 0:
            return 0
        if distance == 4:
            return 7
        return 2 * distance - (0 if direction == "R" else 1)

    def rs_copy(stream, hop):
        k = STREAMS.index(stream) * 4 + hop
        return remote(sbuf.at[k], rbuf.at[k], rs_send.at[k], rs_recv.at[k], z_dev[stream[0]])

    def rs_start(stream):
        direction, sub = stream
        k = STREAMS.index(stream) * 4
        sbuf[k] = pacc[target(direction, REACH[stream]), pl.ds(sub * HALF, HALF), :].astype(BF16)
        rs_copy(stream, 0).start()

    def rs_step(stream, hop):
        direction, sub = stream
        k = STREAMS.index(stream) * 4 + hop
        rs_copy(stream, hop - 1).wait_recv()
        own = pacc[target(direction, REACH[stream] - hop), pl.ds(sub * HALF, HALF), :]
        sbuf[k] = (own + rbuf[k - 1].astype(F32)).astype(BF16)
        rs_copy(stream, hop).start()

    chunk(7)
    rs_start(("R", 0))
    rs_start(("L", 1))
    chunk(6)
    rs_start(("R", 1))
    chunk(5)
    rs_start(("L", 0))
    for o in (4, 3, 2, 1, 0):
        chunk(o)
    for hop in (1, 2, 3):
        for stream in STREAMS:
            if hop < REACH[stream]:
                rs_step(stream, hop)
    for sub in (0, 1):
        rows = pl.ds(sub * HALF, HALF)
        total = pacc[0, rows, :]
        for direction in ("R", "L"):
            stream = (direction, sub)
            k = STREAMS.index(stream) * 4 + REACH[stream] - 1
            rs_copy(stream, REACH[stream] - 1).wait_recv()
            total = total + rbuf[k].astype(F32)
        out[rows, :] = total.astype(BF16)

    for half in (0, 1):
        for stream in STREAMS:
            for distance in range(1, REACH[stream] + 1):
                z_copy(half, stream, distance).wait_send()
        for p in (0, 1):
            for which in range(1, 8):
                kv_copy(piece(0, half, p), 0, half, p, which, partner).wait_send()

    @pl.when(s == 0)
    def _():
        for half in (0, 1):
            for p in (0, 1):
                x_copy(half, p).wait_send()
        for hh in (0, 1):
            wo_share(hh).wait_send()

    @pl.when(s == 1)
    def _():
        for half in (0, 1):
            for copy in q_copies(half):
                copy.wait_send()
        for copy in wo_x_copies():
            copy.wait_send()

    for copy in (*part_copies(0, across), *part_copies(1, across_other), *relay_copies()):
        copy.wait_send()
    for stream in STREAMS:
        for hop in range(REACH[stream]):
            rs_copy(stream, hop).wait_send()


def local(enc_states, dec_states, section_weights, group_lengths):
    dma = pltpu.SemaphoreType.DMA
    vmem = pltpu.VMEM
    return pl.pallas_call(
        kernel,
        out_shape=jax.ShapeDtypeStruct((ROWS, DH), BF16),
        in_specs=[pl.BlockSpec(memory_space=pl.ANY)] * 3 + [pl.BlockSpec(memory_space=pltpu.SMEM)],
        out_specs=pl.BlockSpec(memory_space=pltpu.VMEM),
        scratch_shapes=[
            vmem((NZ, ROWS, FEAT), BF16),
            vmem((2, FEAT, 2, FEAT), BF16),
            vmem((NZ, FEAT, FEAT), BF16),
            vmem((NZ, FEAT, FEAT), BF16),
            vmem((4, FEAT, FEAT), BF16),
            vmem((2, 2, HALF, FEAT), F32),
            vmem((8, 2, GROUP, DH), BF16),
            vmem((8, 2, VROWS, DH), BF16),
            vmem((2, GROUP, DH), BF16),
            vmem((2, VROWS, DH), BF16),
            vmem((2, ROWS, DH), BF16),
            vmem((ROWS, DH), BF16),
            vmem((ROWS, FEAT), BF16),
            vmem((2, ROWS, DH), BF16),
            vmem((2, ROWS, DH), F32),
            vmem((2, ROWS, 128), F32),
            vmem((2, ROWS, 128), F32),
            vmem((2, ROWS, DH), BF16),
            vmem((2, 16, ROWS), F32),
            vmem((3, ROWS, DH), BF16),
            vmem((3, 16, ROWS), F32),
            vmem((NZ, ROWS, DH), F32),
            vmem((16, HALF, DH), BF16),
            vmem((16, HALF, DH), BF16),
            dma((3,)),
            dma((2,)),
            dma((32,)),
            dma((32,)),
            dma((32,)),
            dma((32,)),
            dma((6,)),
            dma((4,)),
            dma((4,)),
            dma((4,)),
            dma((6,)),
            dma((6,)),
            dma((16,)),
            dma((16,)),
        ],
        compiler_params=pltpu.CompilerParams(
            collective_id=0, has_side_effects=True, vmem_limit_bytes=60 * 2**20
        ),
    )(enc_states, dec_states, section_weights, group_lengths)


def solution(mesh):
    in_specs = (P("seq", "mp"), P("seq", "mp"), P("segment", None, None, "mp"), P("seq"))
    out_specs = P("seq", ("segment", "mp"))
    return jax.shard_map(local, mesh=mesh, in_specs=in_specs, out_specs=out_specs, check_vma=False)
```

```python
import jax
import jax.numpy as jnp
from jax import lax
from jax.experimental import pallas as pl
from jax.experimental.pallas import tpu as pltpu
from jax.sharding import PartitionSpec as P

MESH = pl.DeviceIdType.MESH
F32, BF16 = jnp.float32, jnp.bfloat16
DH, GROUP = 256, 128
ROWS, FEAT, NZ = 256, 512, 8
HALF, QUART = ROWS // 2, ROWS // 4
BLOCK = 2 * (GROUP // 2) + 16
NEG = -1e30
DEINT = 32
OFFSETS = (0, -1, 1, -2, 2, -3, 3, 4)
REACH = {("R", 0): 4, ("R", 1): 3, ("L", 1): 4, ("L", 0): 3}
QUARTERS = (0, 1, 2, 3)
STREAMS = (("R", 0), ("L", 1), ("R", 1), ("L", 0))
NT = (((1,), (1,)), ((), ()))


def slot_of(direction, distance):
    if distance == 0:
        return 0
    if distance == 4:
        return 7
    return 2 * distance - (1 if direction == "R" else 0)


def kernel(enc, dec, weights, lengths, out, xg, stage, w0, w1, wo, acc, kv, ks, qbuf, qs, dres, att, oacc,
           mx, den, ps, psm, pr, prm, pacc, sbuf, rbuf, load_sem, stage_sem, z_send, z_recv, kv_send, kv_recv, q_send, q_recv,
           wo_send, wo_recv, p_send, p_recv, rs_send, rs_recv):
    s = lax.axis_index("segment")
    q = lax.axis_index("seq")
    m = lax.axis_index("mp")
    y, xh, c = q // 4, (q // 2) % 2, q % 2
    z_to = {"R": (m + 1) % NZ, "L": (m + NZ - 1) % NZ}

    def seq_of(yy, hh, cc):
        return (yy * 2 + hh) * 2 + cc

    y_up, y_down, y_far = (y + 1) % 4, (y + 3) % 4, (y + 2) % 4
    partner = (s, seq_of(y, xh, 1 - c), m)
    up, down = (s, seq_of(y_up, xh, c), m), (s, seq_of(y_down, xh, c), m)
    across = (1 - s, q, m)
    across_other = (1 - s, seq_of(y, 1 - xh, c), m)
    same_other = (s, seq_of(y, 1 - xh, c), m)
    z_dev = {d: (s, q, z_to[d]) for d in ("R", "L")}

    def remote(src, dst, send, recv, device):
        return pltpu.make_async_remote_copy(
            src_ref=src, dst_ref=dst, send_sem=send, recv_sem=recv, device_id=device, device_id_type=MESH
        )

    def load_x(source):
        return pltpu.make_async_copy(source, xg.at[0], load_sem.at[0])

    @pl.when(s == 0)
    def _():
        load_x(enc).start()

    @pl.when(s == 1)
    def _():
        load_x(dec).start()

    load_res = pltpu.make_async_copy(dec, dres, load_sem.at[1])
    load_res.start()

    def shard_of(o):
        return (m + NZ + OFFSETS[o]) % NZ

    def stage_copy(o):
        rows = pl.ds(pl.multiple_of(shard_of(o) * FEAT, FEAT), FEAT)
        return pltpu.make_async_copy(weights.at[0, rows], stage.at[o % 2], stage_sem.at[o % 2])

    stage_copy(0).start()
    stage_copy(1).start()

    barrier = pltpu.get_barrier_semaphore()
    peers = (z_dev["R"], z_dev["L"], up, down, partner, across, across_other, same_other)
    for peer in peers:
        pl.semaphore_signal(barrier, inc=1, device_id=peer, device_id_type=MESH)
    pl.semaphore_wait(barrier, len(peers))

    def z_copy(r, direction, distance):
        rows = pl.ds(r * QUART, QUART)
        sems = (r * 2 + (direction == "L")) * 4 + distance - 1
        return remote(
            xg.at[slot_of(direction, distance - 1), rows],
            xg.at[slot_of(direction, distance), rows],
            z_send.at[sems],
            z_recv.at[sems],
            z_dev[direction],
        )

    def z_start(*quarters):
        for r in quarters:
            for direction in ("R", "L"):
                z_copy(r, direction, 1).start()

    def z_step(r, distance):
        for direction in ("R", "L"):
            reach = REACH[direction, r % 2]
            if distance <= reach:
                z_copy(r, direction, distance).wait_recv()
                if distance < reach:
                    z_copy(r, direction, distance + 1).start()

    def split(o):
        stage_copy(o).wait()
        j = shard_of(o)

        def body(i, carry):
            r = pl.multiple_of(i * DEINT, DEINT)
            pair = jnp.swapaxes(stage[o % 2, pl.ds(r, DEINT)], 0, 1)
            w0[o, pl.ds(r, DEINT), :] = pair[0]
            w1[j, pl.ds(r, DEINT), :] = pair[1]
            return carry

        lax.fori_loop(0, FEAT // DEINT, body, 0, unroll=2)
        if o + 2 < NZ:
            stage_copy(o + 2).start()

    def project(begin, end, o):
        rows = pl.ds(begin * QUART, (end - begin) * QUART)
        x = xg[o, rows, :]
        first = jnp.dot(x, w0[o], preferred_element_type=F32)
        if o == 0:
            acc[0, rows, :] = first
        else:
            acc[0, rows, :] += first

        @pl.when(s == 0)
        def _():
            second = jnp.dot(x, w1[shard_of(o)], preferred_element_type=F32)
            if o == 0:
                acc[1, rows, :] = second
            else:
                acc[1, rows, :] += second

    def kv_copy(src, index, r, which, device):
        return remote(src, kv.at[index, r], kv_send.at[r * 8 + which], kv_recv.at[r * 8 + index], device)

    def kv_wait(index, r):
        kv_copy(kv.at[index, r], index, r, 0, partner).wait_recv()

    def forward(index, r, which, device):
        kv_copy(kv.at[index, r], index, r, which, device).start()

    def x_copy(r):
        return kv_copy(ks.at[r], y * 2 + c, r, 0, across)

    def q_copies(r):
        rows = pl.ds(r * QUART, QUART)
        return (
            remote(qs.at[rows], qbuf.at[0, rows], q_send.at[r * 3], q_recv.at[r * 2], across),
            remote(qs.at[rows], qbuf.at[1, rows], q_send.at[r * 3 + 1], q_recv.at[r * 2 + 1], across_other),
            remote(qbuf.at[0, rows], qbuf.at[1, rows], q_send.at[r * 3 + 2], q_recv.at[r * 2 + 1], same_other),
        )

    def finish(r):
        rows = pl.ds(r * QUART, QUART)
        own = y * 2 + c

        @pl.when(s == 0)
        def _():
            lane = lax.broadcasted_iota(jnp.int32, (16, DH), 1) - c * QUART
            padding = jnp.logical_and(lane >= 0, lane + (r % 2) * QUART >= lengths[r // 2])
            bias = jnp.where(jnp.logical_and(padding, lane < QUART), NEG, 0.0).astype(BF16)
            ks[r, pl.ds(0, QUART), :] = acc[0, rows, DH:].astype(BF16)
            ks[r, pl.ds(QUART, QUART), :] = acc[1, rows, DH:].astype(BF16)
            ks[r, pl.ds(2 * QUART, 16), :] = bias
            x_copy(r).start()
            kv[own, r, pl.ds(0, QUART), :] = acc[0, rows, :DH].astype(BF16)
            kv[own, r, pl.ds(QUART, QUART), :] = acc[1, rows, :DH].astype(BF16)
            kv[own, r, pl.ds(2 * QUART, 16), :] = bias
            y_near(r, True)

        @pl.when(s == 1)
        def _():
            scale = DH ** -0.5
            qs[rows, :] = acc[0, rows, :DH].astype(BF16) * jnp.asarray(scale, BF16)
            qbuf[0, rows, :] = acc[0, rows, DH:].astype(BF16) * jnp.asarray(scale, BF16)
            for copy in q_copies(r):
                copy.start()

    def y_near(r, local_source):
        index = y * 2 + c
        if not local_source:
            kv_wait(index, r)
        forward(index, r, 1, up)
        forward(index, r, 2, down)
        forward(index, r, 3, partner)

    def y_next(r):
        low, high = y_down * 2 + c, y_up * 2 + c
        one, other = ((low, up, 5, 6), high) if r % 2 == 0 else ((high, down, 6, 5), low)
        index, device, share_one, share_other = one
        kv_wait(index, r)
        forward(index, r, 4, device)
        forward(index, r, share_one, partner)
        kv_wait(other, r)
        forward(other, r, share_other, partner)

    def y_last(r):
        kv_wait(y_far * 2 + c, r)
        forward(y_far * 2 + c, r, 7, partner)

    def shared_wait(r):
        for yy in (y, y_down, y_up, y_far):
            kv_wait(yy * 2 + 1 - c, r)

    def attend(r, k):
        keys = jnp.concatenate([kv[b, r, pl.ds(0, QUART), :] for b in range(8)], axis=0)
        values = jnp.concatenate([kv[b, r, pl.ds(QUART, QUART), :] for b in range(8)], axis=0)
        signs = [kv[b, r, pl.ds(2 * QUART, 16), pl.ds(0, GROUP)].astype(F32)[0:1] for b in range(8)]
        bias = jnp.concatenate([signs[b] + signs[b + 1] for b in range(0, 8, 2)], axis=1)
        best, total = mx[k, :, 0:1], den[k, :, 0:1]
        scores = lax.dot_general(qbuf[k], keys, NT, preferred_element_type=F32) + bias
        new_best = jnp.maximum(best, jnp.max(scores, axis=1, keepdims=True))
        shrink = jnp.exp(best - new_best)
        probs = jnp.exp(scores - new_best).astype(BF16)
        mx[k] = jnp.broadcast_to(new_best, (ROWS, 128))
        den[k] = jnp.broadcast_to(total * shrink + jnp.sum(probs.astype(F32), axis=1, keepdims=True), (ROWS, 128))
        oacc[k] = oacc[k] * shrink + jnp.dot(probs, values, preferred_element_type=F32)

    def part_copies(k, g, device):
        rows = pl.ds(g * HALF, HALF)
        sems = (k * 2 + g) * 2
        return (
            remote(ps.at[k, rows], pr.at[k, rows], p_send.at[sems], p_recv.at[sems], device),
            remote(psm.at[k, g], prm.at[k, g], p_send.at[sems + 1], p_recv.at[sems + 1], device),
        )

    def part_send(k):
        for g in (0, 1):
            rows = pl.ds(g * HALF, HALF)
            ps[k, rows, :] = oacc[k, rows, :].astype(BF16)
            psm[k, g, pl.ds(0, 8), :] = jnp.transpose(mx[k, rows, :])[0:8]
            psm[k, g, pl.ds(8, 8), :] = jnp.transpose(den[k, rows, :])[0:8]
            for copy in part_copies(k, g, across if k == 0 else across_other):
                copy.start()

    def relay_copies(g):
        rows = pl.ds(g * HALF, HALF)
        sems = 8 + 2 * g
        return (
            remote(pr.at[1, rows], pr.at[2, rows], p_send.at[sems], p_recv.at[sems], across),
            remote(prm.at[1, g], prm.at[2, g], p_send.at[sems + 1], p_recv.at[sems + 1], across),
        )

    def column(row):
        return jnp.transpose(jnp.broadcast_to(row, (128, HALF)))[:, 0:1]

    def merge(head, g, one, one_best, one_sum, two, two_best, two_sum):
        best = jnp.maximum(one_best, two_best)
        one_share, two_share = jnp.exp(one_best - best), jnp.exp(two_best - best)
        scale = 1.0 / (one_sum * one_share + two_sum * two_share)
        att[head, pl.ds(g * HALF, HALF), :] = (one * (one_share * scale) + two * (two_share * scale)).astype(BF16)

    def received(slot, g):
        rows = pl.ds(g * HALF, HALF)
        return pr[slot, rows, :].astype(F32), column(prm[slot, g, 0:1, :]), column(prm[slot, g, 8:9, :])

    def part_wait(copies):
        for copy in copies:
            copy.wait_recv()

    part = xh * 2 + c

    def wo_x_copies():
        return (
            remote(w1.at[part], wo.at[part], wo_send.at[0], wo_recv.at[part], across),
            remote(w1.at[part], wo.at[part], wo_send.at[1], wo_recv.at[part], across_other),
        )

    def wo_share(hh):
        index = hh * 2 + c
        return remote(wo.at[index], wo.at[index], wo_send.at[2 + hh], wo_recv.at[index], partner)

    def wo_wait(index):
        remote(wo.at[index], wo.at[index], wo_send.at[0], wo_recv.at[index], partner).wait_recv()

    def wo_local():
        return pltpu.make_async_copy(w1.at[pl.ds(4, 4)], wo, load_sem.at[2])

    @pl.when(s == 0)
    def _():
        load_x(enc).wait()

    @pl.when(s == 1)
    def _():
        load_x(dec).wait()

    def enc_side(body, *args):
        @pl.when(s == 0)
        def _():
            body(*args)

    def dec_side(body, *args):
        @pl.when(s == 1)
        def _():
            body(*args)

    z_start(0, 1, 2)
    mx[...] = jnp.full_like(mx, NEG)
    den[...] = jnp.zeros_like(den)
    oacc[...] = jnp.zeros_like(oacc)
    split(0)
    project(0, 2, 0)
    z_step(0, 1)
    z_step(1, 1)
    z_start(3)
    split(1)
    project(0, 2, 1)
    split(2)
    project(0, 2, 2)
    z_step(2, 1)
    z_step(0, 2)
    z_step(1, 2)
    split(3)
    project(0, 2, 3)
    split(4)
    project(0, 2, 4)
    z_step(3, 1)
    z_step(2, 2)
    z_step(0, 3)
    z_step(1, 3)
    split(5)
    project(0, 2, 5)
    split(6)
    project(0, 2, 6)
    split(7)
    z_step(2, 3)
    z_step(3, 2)
    z_step(0, 4)
    z_step(1, 4)
    project(0, 2, 7)
    finish(0)
    finish(1)

    @pl.when(s == 1)
    def _():
        for copy in wo_x_copies():
            copy.start()
        wo_local().start()

    for o in range(7):
        project(2, 3, o)
    z_step(2, 4)
    z_step(3, 3)
    project(2, 3, 7)
    finish(2)
    for o in range(7):
        project(3, 4, o)
    dec_side(y_near, 0, False)
    dec_side(y_near, 1, False)
    z_step(3, 4)
    project(3, 4, 7)
    finish(3)
    y_next(0)
    dec_side(y_near, 2, False)
    y_next(1)
    dec_side(y_near, 3, False)
    y_next(2)
    y_last(0)
    y_last(1)
    for r in QUARTERS:
        q_copies(r)[1].wait_recv()

    @pl.when(s == 0)
    def _():
        for r in QUARTERS:
            q_copies(r)[0].wait_recv()

    shared_wait(0)
    attend(0, 1)
    attend(0, 0)
    y_next(3)
    shared_wait(1)
    attend(1, 1)
    y_last(2)
    attend(1, 0)
    y_last(3)
    shared_wait(2)
    attend(2, 1)
    attend(2, 0)

    @pl.when(s == 0)
    def _():
        for hh in (0, 1):
            wo_wait(hh * 2 + c)
            wo_share(hh).start()

    shared_wait(3)
    attend(3, 1)
    part_send(1)
    attend(3, 0)
    part_send(0)

    @pl.when(s == 0)
    def _():
        for hh in (0, 1):
            wo_wait(hh * 2 + 1 - c)

    @pl.when(s == 1)
    def _():
        wo_local().wait()

    load_res.wait()

    def chunk(o, g):
        rows = pl.ds(g * HALF, HALF)
        d = shard_of(o)
        block = wo[d // 2, pl.ds(pl.multiple_of((d % 2) * DH, DH), DH), :]
        pacc[o, rows, :] = lax.dot_general(
            att[0, rows, :], block[:, :DH], NT, preferred_element_type=F32
        ) + lax.dot_general(att[1, rows, :], block[:, DH:], NT, preferred_element_type=F32)

        @pl.when(jnp.logical_and(s == m // 4, d // 2 == m % 4))
        def _():
            columns = pl.ds(pl.multiple_of((d % 2) * DH, DH), DH)
            pacc[o, rows, :] += dres[rows, columns].astype(F32)

    def target(direction, distance):
        if distance == 0:
            return 0
        if distance == 4:
            return 7
        return 2 * distance - (0 if direction == "R" else 1)

    def rs_copy(stream, hop):
        k = STREAMS.index(stream) * 4 + hop
        return remote(sbuf.at[k], rbuf.at[k], rs_send.at[k], rs_recv.at[k], z_dev[stream[0]])

    def rs_start(stream):
        direction, sub = stream
        k = STREAMS.index(stream) * 4
        sbuf[k] = pacc[target(direction, REACH[stream]), pl.ds(sub * HALF, HALF), :].astype(BF16)
        rs_copy(stream, 0).start()

    def rs_step(stream, hop):
        direction, sub = stream
        k = STREAMS.index(stream) * 4 + hop
        rs_copy(stream, hop - 1).wait_recv()
        own = pacc[target(direction, REACH[stream] - hop), pl.ds(sub * HALF, HALF), :]
        sbuf[k] = (own + rbuf[k - 1].astype(F32)).astype(BF16)
        rs_copy(stream, hop).start()

    def relay(g):
        part_wait(part_copies(1, g, across_other))
        for copy in relay_copies(g):
            copy.start()

    def gather(g):
        part_wait(part_copies(0, g, across))
        merge(1 - s, g, *received(0, g), *received(1, g))
        part_wait(relay_copies(g))
        rows = pl.ds(g * HALF, HALF)
        merge(s, g, oacc[0, rows, :], mx[0, rows, 0:1], den[0, rows, 0:1], *received(2, g))

    relay(0)
    relay(1)
    gather(0)
    chunk(7, 0)
    rs_start(("R", 0))
    chunk(5, 0)
    rs_start(("L", 0))
    gather(1)
    chunk(7, 1)
    rs_start(("L", 1))
    chunk(6, 1)
    rs_start(("R", 1))
    for o, g in ((6, 0), (3, 0), (5, 1), (4, 1)):
        chunk(o, g)
    rs_step(("R", 0), 1)
    rs_step(("L", 0), 1)
    rs_step(("L", 1), 1)
    rs_step(("R", 1), 1)
    for o, g in ((4, 0), (1, 0), (3, 1), (2, 1)):
        chunk(o, g)
    rs_step(("R", 0), 2)
    rs_step(("L", 0), 2)
    rs_step(("L", 1), 2)
    rs_step(("R", 1), 2)
    for o, g in ((2, 0), (1, 1), (0, 0), (0, 1)):
        chunk(o, g)
    rs_step(("R", 0), 3)
    rs_step(("L", 1), 3)
    for sub in (0, 1):
        rows = pl.ds(sub * HALF, HALF)
        total = pacc[0, rows, :]
        for direction in ("R", "L"):
            stream = (direction, sub)
            k = STREAMS.index(stream) * 4 + REACH[stream] - 1
            rs_copy(stream, REACH[stream] - 1).wait_recv()
            total = total + rbuf[k].astype(F32)
        out[rows, :] = total.astype(BF16)

    for r in QUARTERS:
        for direction in ("R", "L"):
            for distance in range(1, REACH[direction, r % 2] + 1):
                z_copy(r, direction, distance).wait_send()
        for which in range(1, 8):
            kv_copy(kv.at[0, r], 0, r, which, partner).wait_send()

    @pl.when(s == 0)
    def _():
        for r in QUARTERS:
            x_copy(r).wait_send()
        for hh in (0, 1):
            wo_share(hh).wait_send()

    @pl.when(s == 1)
    def _():
        for r in QUARTERS:
            for copy in q_copies(r):
                copy.wait_send()
        for copy in wo_x_copies():
            copy.wait_send()

    for g in (0, 1):
        for copy in (*part_copies(0, g, across), *part_copies(1, g, across_other), *relay_copies(g)):
            copy.wait_send()
    for stream in STREAMS:
        for hop in range(REACH[stream]):
            rs_copy(stream, hop).wait_send()


def local(enc_states, dec_states, section_weights, group_lengths):
    dma = pltpu.SemaphoreType.DMA
    vmem = pltpu.VMEM
    return pl.pallas_call(
        kernel,
        out_shape=jax.ShapeDtypeStruct((ROWS, DH), BF16),
        in_specs=[pl.BlockSpec(memory_space=pl.ANY)] * 3 + [pl.BlockSpec(memory_space=pltpu.SMEM)],
        out_specs=pl.BlockSpec(memory_space=pltpu.VMEM),
        scratch_shapes=[
            vmem((NZ, ROWS, FEAT), BF16),
            vmem((2, FEAT, 2, FEAT), BF16),
            vmem((NZ, FEAT, FEAT), BF16),
            vmem((NZ, FEAT, FEAT), BF16),
            vmem((4, FEAT, FEAT), BF16),
            vmem((2, ROWS, FEAT), F32),
            vmem((8, 4, BLOCK, DH), BF16),
            vmem((4, BLOCK, DH), BF16),
            vmem((2, ROWS, DH), BF16),
            vmem((ROWS, DH), BF16),
            vmem((ROWS, FEAT), BF16),
            vmem((2, ROWS, DH), BF16),
            vmem((2, ROWS, DH), F32),
            vmem((2, ROWS, 128), F32),
            vmem((2, ROWS, 128), F32),
            vmem((2, ROWS, DH), BF16),
            vmem((2, 2, 16, HALF), F32),
            vmem((3, ROWS, DH), BF16),
            vmem((3, 2, 16, HALF), F32),
            vmem((NZ, ROWS, DH), F32),
            vmem((16, HALF, DH), BF16),
            vmem((16, HALF, DH), BF16),
            dma((3,)),
            dma((2,)),
            dma((32,)),
            dma((32,)),
            dma((32,)),
            dma((32,)),
            dma((12,)),
            dma((8,)),
            dma((4,)),
            dma((4,)),
            dma((12,)),
            dma((12,)),
            dma((16,)),
            dma((16,)),
        ],
        compiler_params=pltpu.CompilerParams(
            collective_id=0, has_side_effects=True, vmem_limit_bytes=60 * 2**20
        ),
    )(enc_states, dec_states, section_weights, group_lengths)


def solution(mesh):
    in_specs = (P("seq", "mp"), P("seq", "mp"), P("segment", None, None, "mp"), P("seq"))
    out_specs = P("seq", ("segment", "mp"))
    return jax.shard_map(local, mesh=mesh, in_specs=in_specs, out_specs=out_specs, check_vma=False)
```

```python
import jax
import jax.numpy as jnp
from jax import lax
from jax.experimental import pallas as pl
from jax.experimental.pallas import tpu as pltpu
from jax.sharding import PartitionSpec as P

MESH = pl.DeviceIdType.MESH
F32, BF16 = jnp.float32, jnp.bfloat16
DH, GROUP = 256, 128
ROWS, FEAT, NZ = 256, 512, 8
HALF, QUART = ROWS // 2, ROWS // 4
BLOCK = 2 * (GROUP // 2) + 16
NEG = -1e30
DEINT = 32
OFFSETS = (0, -1, 1, -2, 2, -3, 3, 4)
REACH = {("R", 0): 4, ("R", 1): 3, ("L", 1): 4, ("L", 0): 3}
QUARTERS = (0, 1, 2, 3)
NT = (((1,), (1,)), ((), ()))


def slot_of(direction, distance):
    if distance == 0:
        return 0
    if distance == 4:
        return 7
    return 2 * distance - (1 if direction == "R" else 0)


def kernel(enc, dec, weights, lengths, out, xg, stage, w0, w1, wo, acc, kv, ks, qbuf, qs, dres, att, oacc,
           mx, den, ps, psm, pr, prm, pacc, sbuf, rbuf, load_sem, stage_sem, z_send, z_recv, kv_send, kv_recv, q_send, q_recv,
           wo_send, wo_recv, p_send, p_recv, rs_send, rs_recv):
    s = lax.axis_index("segment")
    q = lax.axis_index("seq")
    m = lax.axis_index("mp")
    y, xh, c = q // 4, (q // 2) % 2, q % 2
    z_to = {"R": (m + 1) % NZ, "L": (m + NZ - 1) % NZ}

    def seq_of(yy, hh, cc):
        return (yy * 2 + hh) * 2 + cc

    y_up, y_down, y_far = (y + 1) % 4, (y + 3) % 4, (y + 2) % 4
    partner = (s, seq_of(y, xh, 1 - c), m)
    up, down = (s, seq_of(y_up, xh, c), m), (s, seq_of(y_down, xh, c), m)
    across = (1 - s, q, m)
    across_other = (1 - s, seq_of(y, 1 - xh, c), m)
    same_other = (s, seq_of(y, 1 - xh, c), m)
    z_dev = {d: (s, q, z_to[d]) for d in ("R", "L")}

    def remote(src, dst, send, recv, device):
        return pltpu.make_async_remote_copy(
            src_ref=src, dst_ref=dst, send_sem=send, recv_sem=recv, device_id=device, device_id_type=MESH
        )

    def load_x(source):
        return pltpu.make_async_copy(source, xg.at[0], load_sem.at[0])

    @pl.when(s == 0)
    def _():
        load_x(enc).start()

    @pl.when(s == 1)
    def _():
        load_x(dec).start()

    load_res = pltpu.make_async_copy(dec, dres, load_sem.at[1])
    load_res.start()

    def shard_of(o):
        return (m + NZ + OFFSETS[o]) % NZ

    def stage_copy(o):
        rows = pl.ds(pl.multiple_of(shard_of(o) * FEAT, FEAT), FEAT)
        return pltpu.make_async_copy(weights.at[0, rows], stage.at[o % 2], stage_sem.at[o % 2])

    stage_copy(0).start()
    stage_copy(1).start()

    barrier = pltpu.get_barrier_semaphore()
    peers = (z_dev["R"], z_dev["L"], up, down, partner, across, across_other, same_other)
    for peer in peers:
        pl.semaphore_signal(barrier, inc=1, device_id=peer, device_id_type=MESH)
    pl.semaphore_wait(barrier, len(peers))

    def z_copy(r, direction, distance):
        rows = pl.ds(r * QUART, QUART)
        sems = (r * 2 + (direction == "L")) * 4 + distance - 1
        return remote(
            xg.at[slot_of(direction, distance - 1), rows],
            xg.at[slot_of(direction, distance), rows],
            z_send.at[sems],
            z_recv.at[sems],
            z_dev[direction],
        )

    def z_start(*quarters):
        for r in quarters:
            for direction in ("R", "L"):
                z_copy(r, direction, 1).start()

    def z_step(r, distance):
        for direction in ("R", "L"):
            reach = REACH[direction, r % 2]
            if distance <= reach:
                z_copy(r, direction, distance).wait_recv()
                if distance < reach:
                    z_copy(r, direction, distance + 1).start()

    def split(o):
        stage_copy(o).wait()
        j = shard_of(o)

        def body(i, carry):
            r = pl.multiple_of(i * DEINT, DEINT)
            pair = jnp.swapaxes(stage[o % 2, pl.ds(r, DEINT)], 0, 1)
            w0[o, pl.ds(r, DEINT), :] = pair[0]
            w1[j, pl.ds(r, DEINT), :] = pair[1]
            return carry

        lax.fori_loop(0, FEAT // DEINT, body, 0, unroll=2)
        if o + 2 < NZ:
            stage_copy(o + 2).start()

    def project(begin, end, o):
        rows = pl.ds(begin * QUART, (end - begin) * QUART)
        x = xg[o, rows, :]
        first = jnp.dot(x, w0[o], preferred_element_type=F32)
        if o == 0:
            acc[0, rows, :] = first
        else:
            acc[0, rows, :] += first

        @pl.when(s == 0)
        def _():
            second = jnp.dot(x, w1[shard_of(o)], preferred_element_type=F32)
            if o == 0:
                acc[1, rows, :] = second
            else:
                acc[1, rows, :] += second

    def kv_copy(src, index, r, which, device):
        return remote(src, kv.at[index, r], kv_send.at[r * 8 + which], kv_recv.at[r * 8 + index], device)

    def kv_wait(index, r):
        kv_copy(kv.at[index, r], index, r, 0, partner).wait_recv()

    def forward(index, r, which, device):
        kv_copy(kv.at[index, r], index, r, which, device).start()

    def x_copy(r):
        return kv_copy(ks.at[r], y * 2 + c, r, 0, across)

    def q_copies(r):
        rows = pl.ds(r * QUART, QUART)
        return (
            remote(qs.at[rows], qbuf.at[0, rows], q_send.at[r * 3], q_recv.at[r * 2], across),
            remote(qs.at[rows], qbuf.at[1, rows], q_send.at[r * 3 + 1], q_recv.at[r * 2 + 1], across_other),
            remote(qbuf.at[0, rows], qbuf.at[1, rows], q_send.at[r * 3 + 2], q_recv.at[r * 2 + 1], same_other),
        )

    def finish(r):
        rows = pl.ds(r * QUART, QUART)
        own = y * 2 + c

        @pl.when(s == 0)
        def _():
            lane = lax.broadcasted_iota(jnp.int32, (16, DH), 1) - c * QUART
            padding = jnp.logical_and(lane >= 0, lane + (r % 2) * QUART >= lengths[r // 2])
            bias = jnp.where(jnp.logical_and(padding, lane < QUART), NEG, 0.0).astype(BF16)
            ks[r, pl.ds(0, QUART), :] = acc[0, rows, DH:].astype(BF16)
            ks[r, pl.ds(QUART, QUART), :] = acc[1, rows, DH:].astype(BF16)
            ks[r, pl.ds(2 * QUART, 16), :] = bias
            x_copy(r).start()
            kv[own, r, pl.ds(0, QUART), :] = acc[0, rows, :DH].astype(BF16)
            kv[own, r, pl.ds(QUART, QUART), :] = acc[1, rows, :DH].astype(BF16)
            kv[own, r, pl.ds(2 * QUART, 16), :] = bias
            y_near(r, True)

        @pl.when(s == 1)
        def _():
            scale = DH ** -0.5
            qs[rows, :] = acc[0, rows, :DH].astype(BF16) * jnp.asarray(scale, BF16)
            qbuf[0, rows, :] = acc[0, rows, DH:].astype(BF16) * jnp.asarray(scale, BF16)
            for copy in q_copies(r):
                copy.start()

    def y_near(r, local_source):
        index = y * 2 + c
        if not local_source:
            kv_wait(index, r)
        forward(index, r, 1, up)
        forward(index, r, 2, down)
        forward(index, r, 3, partner)

    def y_next(r):
        low, high = y_down * 2 + c, y_up * 2 + c
        one, other = ((low, up, 5, 6), high) if r % 2 == 0 else ((high, down, 6, 5), low)
        index, device, share_one, share_other = one
        kv_wait(index, r)
        forward(index, r, 4, device)
        forward(index, r, share_one, partner)
        kv_wait(other, r)
        forward(other, r, share_other, partner)

    def y_last(r):
        kv_wait(y_far * 2 + c, r)
        forward(y_far * 2 + c, r, 7, partner)

    def shared_wait(r):
        for yy in (y, y_down, y_up, y_far):
            kv_wait(yy * 2 + 1 - c, r)

    def attend(r, k):
        keys = jnp.concatenate([kv[b, r, pl.ds(0, QUART), :] for b in range(8)], axis=0)
        values = jnp.concatenate([kv[b, r, pl.ds(QUART, QUART), :] for b in range(8)], axis=0)
        signs = [kv[b, r, pl.ds(2 * QUART, 16), pl.ds(0, GROUP)].astype(F32)[0:1] for b in range(8)]
        bias = jnp.concatenate([signs[b] + signs[b + 1] for b in range(0, 8, 2)], axis=1)
        best, total = mx[k, :, 0:1], den[k, :, 0:1]
        scores = lax.dot_general(qbuf[k], keys, NT, preferred_element_type=F32) + bias
        new_best = jnp.maximum(best, jnp.max(scores, axis=1, keepdims=True))
        shrink = jnp.exp(best - new_best)
        probs = jnp.exp(scores - new_best).astype(BF16)
        mx[k] = jnp.broadcast_to(new_best, (ROWS, 128))
        den[k] = jnp.broadcast_to(total * shrink + jnp.sum(probs.astype(F32), axis=1, keepdims=True), (ROWS, 128))
        oacc[k] = oacc[k] * shrink + jnp.dot(probs, values, preferred_element_type=F32)

    def part_copies(k, g, device):
        rows = pl.ds(g * QUART, QUART)
        data = remote(ps.at[k, rows], pr.at[k, rows], p_send.at[k * 6 + g], p_recv.at[k * 6 + g], device)
        if g % 2:
            return (data,)
        n = k * 6 + 4 + g // 2
        return (remote(psm.at[k, g // 2], prm.at[k, g // 2], p_send.at[n], p_recv.at[n], device), data)

    def part_send(k):
        for g in QUARTERS:
            rows = pl.ds(g * QUART, QUART)
            ps[k, rows, :] = oacc[k, rows, :].astype(BF16)
            if g % 2 == 0:
                both = pl.ds(g * QUART, HALF)
                psm[k, g // 2, pl.ds(0, 8), :] = jnp.transpose(mx[k, both, :])[0:8]
                psm[k, g // 2, pl.ds(8, 8), :] = jnp.transpose(den[k, both, :])[0:8]
            for copy in part_copies(k, g, across if k == 0 else across_other):
                copy.start()

    def relay_copies(g):
        rows = pl.ds(g * QUART, QUART)
        data = remote(pr.at[1, rows], pr.at[2, rows], p_send.at[12 + g], p_recv.at[12 + g], across)
        if g % 2:
            return (data,)
        n = 16 + g // 2
        return (remote(prm.at[1, g // 2], prm.at[2, g // 2], p_send.at[n], p_recv.at[n], across), data)

    def column(row):
        return jnp.transpose(jnp.broadcast_to(row, (128, HALF)))[:, 0:1]

    def merge(head, g, one, one_best, one_sum, two, two_best, two_sum):
        best = jnp.maximum(one_best, two_best)
        one_share, two_share = jnp.exp(one_best - best), jnp.exp(two_best - best)
        scale = 1.0 / (one_sum * one_share + two_sum * two_share)
        att[head, pl.ds(g * HALF, HALF), :] = (one * (one_share * scale) + two * (two_share * scale)).astype(BF16)

    def received(slot, g):
        rows = pl.ds(g * HALF, HALF)
        return pr[slot, rows, :].astype(F32), column(prm[slot, g, 0:1, :]), column(prm[slot, g, 8:9, :])

    def part_wait(copies):
        for copy in copies:
            copy.wait_recv()

    part = xh * 2 + c

    def wo_x_copies():
        return (
            remote(w1.at[part], wo.at[part], wo_send.at[0], wo_recv.at[part], across),
            remote(w1.at[part], wo.at[part], wo_send.at[1], wo_recv.at[part], across_other),
        )

    def wo_share(hh):
        index = hh * 2 + c
        return remote(wo.at[index], wo.at[index], wo_send.at[2 + hh], wo_recv.at[index], partner)

    def wo_wait(index):
        remote(wo.at[index], wo.at[index], wo_send.at[0], wo_recv.at[index], partner).wait_recv()

    def wo_local():
        return pltpu.make_async_copy(w1.at[pl.ds(4, 4)], wo, load_sem.at[2])

    @pl.when(s == 0)
    def _():
        load_x(enc).wait()

    @pl.when(s == 1)
    def _():
        load_x(dec).wait()

    def enc_side(body, *args):
        @pl.when(s == 0)
        def _():
            body(*args)

    def dec_side(body, *args):
        @pl.when(s == 1)
        def _():
            body(*args)

    z_start(0, 1)
    mx[...] = jnp.full_like(mx, NEG)
    den[...] = jnp.zeros_like(den)
    oacc[...] = jnp.zeros_like(oacc)
    split(0)
    split(1)
    project(0, 2, 0)
    z_step(0, 1)
    z_step(1, 1)
    z_start(2, 3)
    split(2)
    split(3)
    project(0, 2, 1)
    project(0, 2, 2)
    z_step(0, 2)
    z_step(1, 2)
    split(4)
    split(5)
    project(0, 2, 3)
    project(0, 2, 4)
    z_step(2, 1)
    z_step(3, 1)
    split(6)
    split(7)

    @pl.when(s == 1)
    def _():
        for copy in wo_x_copies():
            copy.start()
        wo_local().start()

    z_step(0, 3)
    z_step(1, 3)
    z_step(2, 2)
    z_step(3, 2)
    project(0, 2, 5)
    project(0, 2, 6)
    z_step(0, 4)
    z_step(1, 4)
    project(0, 2, 7)
    finish(0)
    finish(1)
    project(2, 4, 0)
    project(2, 4, 1)
    project(2, 4, 2)
    project(2, 4, 3)
    z_step(2, 3)
    z_step(3, 3)
    project(2, 4, 4)
    project(2, 4, 5)
    project(2, 4, 6)
    dec_side(y_near, 0, False)
    dec_side(y_near, 1, False)
    z_step(2, 4)
    z_step(3, 4)
    project(2, 4, 7)
    finish(2)
    finish(3)
    y_next(0)
    dec_side(y_near, 2, False)
    y_next(1)
    dec_side(y_near, 3, False)
    y_next(2)
    y_last(0)
    y_last(1)
    for r in QUARTERS:
        q_copies(r)[1].wait_recv()

    @pl.when(s == 0)
    def _():
        for r in QUARTERS:
            q_copies(r)[0].wait_recv()

    shared_wait(0)
    attend(0, 1)
    attend(0, 0)
    y_next(3)
    shared_wait(1)
    attend(1, 1)
    y_last(2)
    attend(1, 0)
    y_last(3)
    shared_wait(2)
    attend(2, 1)
    attend(2, 0)

    @pl.when(s == 0)
    def _():
        for hh in (0, 1):
            wo_wait(hh * 2 + c)
            wo_share(hh).start()

    shared_wait(3)
    attend(3, 1)
    part_send(1)
    attend(3, 0)
    part_send(0)

    @pl.when(s == 0)
    def _():
        for hh in (0, 1):
            wo_wait(hh * 2 + 1 - c)

    @pl.when(s == 1)
    def _():
        wo_local().wait()

    load_res.wait()

    def chunk(o, g):
        rows = pl.ds(g * HALF, HALF)
        d = shard_of(o)
        block = wo[d // 2, pl.ds(pl.multiple_of((d % 2) * DH, DH), DH), :]
        pacc[o, rows, :] = lax.dot_general(
            att[0, rows, :], block[:, :DH], NT, preferred_element_type=F32
        ) + lax.dot_general(att[1, rows, :], block[:, DH:], NT, preferred_element_type=F32)

        @pl.when(jnp.logical_and(s == m // 4, d // 2 == m % 4))
        def _():
            columns = pl.ds(pl.multiple_of((d % 2) * DH, DH), DH)
            pacc[o, rows, :] += dres[rows, columns].astype(F32)

    def target(direction, distance):
        if distance == 0:
            return 0
        if distance == 4:
            return 7
        return 2 * distance - (0 if direction == "R" else 1)

    def rs_copy(direction, r, hop):
        k = (r * 2 + (direction == "L")) * 4 + hop
        return remote(sbuf.at[k], rbuf.at[k], rs_send.at[k], rs_recv.at[k], z_dev[direction])

    def rs_start(direction, r):
        k = (r * 2 + (direction == "L")) * 4
        sbuf[k] = pacc[target(direction, REACH[direction, r % 2]), pl.ds(r * QUART, QUART), :].astype(BF16)
        rs_copy(direction, r, 0).start()

    def rs_step(hop, *quarters):
        for r in quarters:
            for direction in ("R", "L") if r % 2 == 0 else ("L", "R"):
                reach = REACH[direction, r % 2]
                if hop < reach:
                    k = (r * 2 + (direction == "L")) * 4 + hop
                    rs_copy(direction, r, hop - 1).wait_recv()
                    own = pacc[target(direction, reach - hop), pl.ds(r * QUART, QUART), :]
                    sbuf[k] = (own + rbuf[k - 1].astype(F32)).astype(BF16)
                    rs_copy(direction, r, hop).start()

    def relay(g):
        part_wait(part_copies(1, g, across_other))
        for copy in relay_copies(g):
            copy.start()

    def gather(g):
        for r in (2 * g, 2 * g + 1):
            part_wait(part_copies(0, r, across))
        merge(1 - s, g, *received(0, g), *received(1, g))
        for r in (2 * g, 2 * g + 1):
            part_wait(relay_copies(r))
        rows = pl.ds(g * HALF, HALF)
        merge(s, g, oacc[0, rows, :], mx[0, rows, 0:1], den[0, rows, 0:1], *received(2, g))

    for g in QUARTERS:
        relay(g)
    for g in (0, 1):
        gather(g)
        chunk(7, g)
        rs_start("R", 2 * g)
        rs_start("L", 2 * g + 1)
        chunk(5, g)
        rs_start("L", 2 * g)
        chunk(6, g)
        rs_start("R", 2 * g + 1)
    chunk(3, 0)
    chunk(4, 0)
    rs_step(1, 0, 1)
    chunk(3, 1)
    chunk(4, 1)
    rs_step(1, 2, 3)
    chunk(1, 0)
    chunk(2, 0)
    rs_step(2, 0, 1)
    chunk(1, 1)
    chunk(2, 1)
    rs_step(2, 2, 3)
    chunk(0, 0)
    rs_step(3, 0, 1)
    chunk(0, 1)
    rs_step(3, 2, 3)
    for r in QUARTERS:
        rows = pl.ds(r * QUART, QUART)
        total = pacc[0, rows, :]
        for direction in ("R", "L") if r % 2 else ("L", "R"):
            hop = REACH[direction, r % 2] - 1
            rs_copy(direction, r, hop).wait_recv()
            total = total + rbuf[(r * 2 + (direction == "L")) * 4 + hop].astype(F32)
        out[rows, :] = total.astype(BF16)

    for r in QUARTERS:
        for direction in ("R", "L"):
            for distance in range(1, REACH[direction, r % 2] + 1):
                z_copy(r, direction, distance).wait_send()
        for which in range(1, 8):
            kv_copy(kv.at[0, r], 0, r, which, partner).wait_send()

    @pl.when(s == 0)
    def _():
        for r in QUARTERS:
            x_copy(r).wait_send()
        for hh in (0, 1):
            wo_share(hh).wait_send()

    @pl.when(s == 1)
    def _():
        for r in QUARTERS:
            for copy in q_copies(r):
                copy.wait_send()
        for copy in wo_x_copies():
            copy.wait_send()

    for r in QUARTERS:
        for copy in (*part_copies(0, r, across), *part_copies(1, r, across_other), *relay_copies(r)):
            copy.wait_send()
        for direction in ("R", "L"):
            for hop in range(REACH[direction, r % 2]):
                rs_copy(direction, r, hop).wait_send()


def local(enc_states, dec_states, section_weights, group_lengths):
    dma = pltpu.SemaphoreType.DMA
    vmem = pltpu.VMEM
    return pl.pallas_call(
        kernel,
        out_shape=jax.ShapeDtypeStruct((ROWS, DH), BF16),
        in_specs=[pl.BlockSpec(memory_space=pl.ANY)] * 3 + [pl.BlockSpec(memory_space=pltpu.SMEM)],
        out_specs=pl.BlockSpec(memory_space=pltpu.VMEM),
        scratch_shapes=[
            vmem((NZ, ROWS, FEAT), BF16),
            vmem((2, FEAT, 2, FEAT), BF16),
            vmem((NZ, FEAT, FEAT), BF16),
            vmem((NZ, FEAT, FEAT), BF16),
            vmem((4, FEAT, FEAT), BF16),
            vmem((2, ROWS, FEAT), F32),
            vmem((8, 4, BLOCK, DH), BF16),
            vmem((4, BLOCK, DH), BF16),
            vmem((2, ROWS, DH), BF16),
            vmem((ROWS, DH), BF16),
            vmem((ROWS, FEAT), BF16),
            vmem((2, ROWS, DH), BF16),
            vmem((2, ROWS, DH), F32),
            vmem((2, ROWS, 128), F32),
            vmem((2, ROWS, 128), F32),
            vmem((2, ROWS, DH), BF16),
            vmem((2, 2, 16, HALF), F32),
            vmem((3, ROWS, DH), BF16),
            vmem((3, 2, 16, HALF), F32),
            vmem((NZ, ROWS, DH), F32),
            vmem((32, QUART, DH), BF16),
            vmem((32, QUART, DH), BF16),
            dma((3,)),
            dma((2,)),
            dma((32,)),
            dma((32,)),
            dma((32,)),
            dma((32,)),
            dma((12,)),
            dma((8,)),
            dma((4,)),
            dma((4,)),
            dma((18,)),
            dma((18,)),
            dma((32,)),
            dma((32,)),
        ],
        compiler_params=pltpu.CompilerParams(
            collective_id=0, has_side_effects=True, vmem_limit_bytes=60 * 2**20
        ),
    )(enc_states, dec_states, section_weights, group_lengths)


def solution(mesh):
    in_specs = (P("seq", "mp"), P("seq", "mp"), P("segment", None, None, "mp"), P("seq"))
    out_specs = P("seq", ("segment", "mp"))
    return jax.shard_map(local, mesh=mesh, in_specs=in_specs, out_specs=out_specs, check_vma=False)
```

```python
import jax
import jax.numpy as jnp
from jax import lax
from jax.experimental import pallas as pl
from jax.experimental.pallas import tpu as pltpu
from jax.sharding import PartitionSpec as P

MESH = pl.DeviceIdType.MESH
F32, BF16 = jnp.float32, jnp.bfloat16
DH, GROUP = 256, 128
ROWS, FEAT, NZ = 256, 512, 8
HALF, QUART = ROWS // 2, ROWS // 4
BLOCK = 2 * (GROUP // 2) + 16
NEG = -1e30
DEINT = 32
OFFSETS = (0, -1, 1, -2, 2, -3, 3, 4)
REACH = {("R", 0): 4, ("R", 1): 3, ("L", 1): 4, ("L", 0): 3}
QUARTERS = (0, 1, 2, 3)
NT = (((1,), (1,)), ((), ()))


def slot_of(direction, distance):
    if distance == 0:
        return 0
    if distance == 4:
        return 7
    return 2 * distance - (1 if direction == "R" else 0)


def kernel(enc, dec, weights, lengths, out, xg, stage, w0, w1, wo, acc, kv, ks, qbuf, qs, dres, att, oacc,
           mx, den, pacc, sbuf, rbuf, load_sem, stage_sem, z_send, z_recv, kv_send, kv_recv, q_send, q_recv,
           wo_send, wo_recv, p_send, p_recv, rs_send, rs_recv):
    s = lax.axis_index("segment")
    q = lax.axis_index("seq")
    m = lax.axis_index("mp")
    y, xh, c = q // 4, (q // 2) % 2, q % 2
    z_to = {"R": (m + 1) % NZ, "L": (m + NZ - 1) % NZ}

    def seq_of(yy, hh, cc):
        return (yy * 2 + hh) * 2 + cc

    y_up, y_down, y_far = (y + 1) % 4, (y + 3) % 4, (y + 2) % 4
    partner = (s, seq_of(y, xh, 1 - c), m)
    up, down = (s, seq_of(y_up, xh, c), m), (s, seq_of(y_down, xh, c), m)
    across = (1 - s, q, m)
    across_other = (1 - s, seq_of(y, 1 - xh, c), m)
    same_other = (s, seq_of(y, 1 - xh, c), m)
    z_dev = {d: (s, q, z_to[d]) for d in ("R", "L")}

    def remote(src, dst, send, recv, device):
        return pltpu.make_async_remote_copy(
            src_ref=src, dst_ref=dst, send_sem=send, recv_sem=recv, device_id=device, device_id_type=MESH
        )

    def load_x(source):
        return pltpu.make_async_copy(source, xg.at[0], load_sem.at[0])

    @pl.when(s == 0)
    def _():
        load_x(enc).start()

    @pl.when(s == 1)
    def _():
        load_x(dec).start()

    load_res = pltpu.make_async_copy(dec, dres, load_sem.at[1])
    load_res.start()

    def shard_of(o):
        return (m + NZ + OFFSETS[o]) % NZ

    def stage_copy(o):
        rows = pl.ds(pl.multiple_of(shard_of(o) * FEAT, FEAT), FEAT)
        return pltpu.make_async_copy(weights.at[0, rows], stage.at[o % 2], stage_sem.at[o % 2])

    stage_copy(0).start()
    stage_copy(1).start()

    barrier = pltpu.get_barrier_semaphore()
    peers = (z_dev["R"], z_dev["L"], up, down, partner, across, across_other, same_other)
    for peer in peers:
        pl.semaphore_signal(barrier, inc=1, device_id=peer, device_id_type=MESH)
    pl.semaphore_wait(barrier, len(peers))

    def z_copy(r, direction, distance):
        rows = pl.ds(r * QUART, QUART)
        sems = (r * 2 + (direction == "L")) * 4 + distance - 1
        return remote(
            xg.at[slot_of(direction, distance - 1), rows],
            xg.at[slot_of(direction, distance), rows],
            z_send.at[sems],
            z_recv.at[sems],
            z_dev[direction],
        )

    def z_start(*quarters):
        for r in quarters:
            for direction in ("R", "L"):
                z_copy(r, direction, 1).start()

    def z_step(r, distance):
        for direction in ("R", "L"):
            reach = REACH[direction, r % 2]
            if distance <= reach:
                z_copy(r, direction, distance).wait_recv()
                if distance < reach:
                    z_copy(r, direction, distance + 1).start()

    def split(o):
        stage_copy(o).wait()
        j = shard_of(o)

        def body(i, carry):
            r = pl.multiple_of(i * DEINT, DEINT)
            pair = jnp.swapaxes(stage[o % 2, pl.ds(r, DEINT)], 0, 1)
            w0[o, pl.ds(r, DEINT), :] = pair[0]
            w1[j, pl.ds(r, DEINT), :] = pair[1]
            return carry

        lax.fori_loop(0, FEAT // DEINT, body, 0, unroll=2)
        if o + 2 < NZ:
            stage_copy(o + 2).start()

    def project(begin, end, o):
        rows = pl.ds(begin * QUART, (end - begin) * QUART)
        x = xg[o, rows, :]
        first = jnp.dot(x, w0[o], preferred_element_type=F32)
        if o == 0:
            acc[0, rows, :] = first
        else:
            acc[0, rows, :] += first

        @pl.when(s == 0)
        def _():
            second = jnp.dot(x, w1[shard_of(o)], preferred_element_type=F32)
            if o == 0:
                acc[1, rows, :] = second
            else:
                acc[1, rows, :] += second

    def kv_copy(src, source, r, which, device):
        return remote(src, kv.at[source, r], kv_send.at[r * 17 + which], kv_recv.at[r * 16 + source], device)

    def kv_wait(source, r):
        kv_copy(kv.at[source, r], source, r, 0, partner).wait_recv()

    def forward(source, r, which, device):
        kv_copy(kv.at[source, r], source, r, which, device).start()

    def x_copies(r):
        return (
            kv_copy(ks.at[r], q, r, 0, across_other),
            kv_copy(kv.at[q, r], q, r, 1, same_other),
            kv_copy(ks.at[r], q, r, 2, across),
        )

    def q_copy(r):
        rows = pl.ds(r * QUART, QUART)
        return remote(qs.at[rows], qbuf.at[rows], q_send.at[r], q_recv.at[r], across)

    def finish(r):
        rows = pl.ds(r * QUART, QUART)

        @pl.when(s == 0)
        def _():
            lane = lax.broadcasted_iota(jnp.int32, (16, DH), 1) - c * QUART
            padding = jnp.logical_and(lane >= 0, lane + (r % 2) * QUART >= lengths[r // 2])
            bias = jnp.where(jnp.logical_and(padding, lane < QUART), NEG, 0.0).astype(BF16)
            ks[r, pl.ds(0, QUART), :] = acc[0, rows, DH:].astype(BF16)
            ks[r, pl.ds(QUART, QUART), :] = acc[1, rows, DH:].astype(BF16)
            ks[r, pl.ds(2 * QUART, 16), :] = bias
            kv[q, r, pl.ds(0, QUART), :] = acc[0, rows, :DH].astype(BF16)
            kv[q, r, pl.ds(QUART, QUART), :] = acc[1, rows, :DH].astype(BF16)
            kv[q, r, pl.ds(2 * QUART, 16), :] = bias
            for copy in x_copies(r):
                copy.start()
            y_near(r, 0, True)

        @pl.when(s == 1)
        def _():
            scale = DH ** -0.5
            qs[rows, :] = acc[0, rows, :DH].astype(BF16) * jnp.asarray(scale, BF16)
            qbuf[rows, :] = acc[0, rows, DH:].astype(BF16) * jnp.asarray(scale, BF16)
            q_copy(r).start()

    def source_of(yy, k):
        return seq_of(yy, xh if k == 0 else 1 - xh, c)

    def y_near(r, k, local_source):
        source = source_of(y, k)
        if not local_source:
            kv_wait(source, r)
        forward(source, r, 3 + 2 * k, up)
        forward(source, r, 4 + 2 * k, down)
        forward(source, r, 8 + k, partner)

    def y_next(r, k):
        low, high = source_of(y_down, k), source_of(y_up, k)
        one, device, share, other, other_share = (
            (low, up, 11 + k, high, 13 + k) if (r + k) % 2 == 0 else (high, down, 13 + k, low, 11 + k)
        )
        kv_wait(one, r)
        forward(one, r, 7 if k == 0 else 10, device)
        forward(one, r, share, partner)
        kv_wait(other, r)
        forward(other, r, other_share, partner)

    def y_last(r, k):
        kv_wait(source_of(y_far, k), r)
        forward(source_of(y_far, k), r, 15 + k, partner)

    def shared_wait(r):
        for yy in (y, y_down, y_up, y_far):
            for hh in (0, 1):
                kv_wait(seq_of(yy, hh, 1 - c), r)

    def attend(r):
        for first in (0, 8):
            blocks = range(first, first + 8)
            keys = jnp.concatenate([kv[b, r, pl.ds(0, QUART), :] for b in blocks], axis=0)
            values = jnp.concatenate([kv[b, r, pl.ds(QUART, QUART), :] for b in blocks], axis=0)
            signs = [kv[b, r, pl.ds(2 * QUART, 16), pl.ds(0, GROUP)].astype(F32)[0:1] for b in blocks]
            bias = jnp.concatenate([signs[b] + signs[b + 1] for b in range(0, 8, 2)], axis=1)
            best, total = mx[:, 0:1], den[:, 0:1]
            scores = lax.dot_general(qbuf[...], keys, NT, preferred_element_type=F32) + bias
            new_best = jnp.maximum(best, jnp.max(scores, axis=1, keepdims=True))
            shrink = jnp.exp(best - new_best)
            probs = jnp.exp(scores - new_best).astype(BF16)
            mx[:, 0:1] = new_best
            den[:, 0:1] = total * shrink + jnp.sum(probs.astype(F32), axis=1, keepdims=True)
            oacc[...] = oacc[...] * shrink + jnp.dot(probs, values, preferred_element_type=F32)

    def att_copy(head, r):
        rows = pl.ds(r * QUART, QUART)
        return remote(att.at[head, rows], att.at[head, rows], p_send.at[r], p_recv.at[r], across)

    part = xh * 2 + c

    def wo_x_copies():
        return (
            remote(w1.at[part], wo.at[part], wo_send.at[0], wo_recv.at[part], across),
            remote(w1.at[part], wo.at[part], wo_send.at[1], wo_recv.at[part], across_other),
        )

    def wo_share(hh):
        index = hh * 2 + c
        return remote(wo.at[index], wo.at[index], wo_send.at[2 + hh], wo_recv.at[index], partner)

    def wo_wait(index):
        remote(wo.at[index], wo.at[index], wo_send.at[0], wo_recv.at[index], partner).wait_recv()

    def wo_local():
        return pltpu.make_async_copy(w1.at[pl.ds(4, 4)], wo, load_sem.at[2])

    @pl.when(s == 0)
    def _():
        load_x(enc).wait()

    @pl.when(s == 1)
    def _():
        load_x(dec).wait()

    def enc_side(body, *args):
        @pl.when(s == 0)
        def _():
            body(*args)

    def dec_side(body, *args):
        @pl.when(s == 1)
        def _():
            body(*args)

    z_start(0, 1)
    mx[...] = jnp.full_like(mx, NEG)
    den[...] = jnp.zeros_like(den)
    oacc[...] = jnp.zeros_like(oacc)
    split(0)
    split(1)
    project(0, 2, 0)
    z_step(0, 1)
    z_step(1, 1)
    z_start(2, 3)
    split(2)
    split(3)
    project(0, 2, 1)
    project(0, 2, 2)
    z_step(0, 2)
    z_step(1, 2)
    split(4)
    split(5)
    project(0, 2, 3)
    project(0, 2, 4)
    z_step(2, 1)
    z_step(3, 1)
    split(6)
    split(7)

    @pl.when(s == 1)
    def _():
        for copy in wo_x_copies():
            copy.start()
        wo_local().start()

    z_step(0, 3)
    z_step(1, 3)
    z_step(2, 2)
    z_step(3, 2)
    project(0, 2, 5)
    project(0, 2, 6)
    z_step(0, 4)
    z_step(1, 4)
    project(0, 2, 7)
    finish(0)
    finish(1)
    project(2, 4, 0)
    project(2, 4, 1)
    project(2, 4, 2)
    project(2, 4, 3)
    z_step(2, 3)
    z_step(3, 3)
    project(2, 4, 4)
    project(2, 4, 5)
    project(2, 4, 6)
    dec_side(y_near, 0, 0, False)
    dec_side(y_near, 0, 1, False)
    z_step(2, 4)
    z_step(3, 4)
    project(2, 4, 7)
    finish(2)
    finish(3)
    for k in (0, 1):
        dec_side(y_near, 1, k, False)
    y_next(0, 0)
    enc_side(y_near, 0, 1, False)
    y_next(1, 0)
    enc_side(y_near, 1, 1, False)
    y_next(0, 1)
    for k in (0, 1):
        dec_side(y_near, 2, k, False)
    y_next(1, 1)
    y_last(0, 0)
    y_last(1, 0)
    enc_side(y_near, 2, 1, False)
    y_next(2, 0)
    y_last(0, 1)
    for k in (0, 1):
        dec_side(y_near, 3, k, False)
    enc_side(y_near, 3, 1, False)
    y_last(1, 1)

    @pl.when(s == 0)
    def _():
        for r in QUARTERS:
            q_copy(r).wait_recv()

    shared_wait(0)
    attend(0)
    y_next(2, 1)
    y_next(3, 0)
    shared_wait(1)
    attend(1)
    y_next(3, 1)
    y_last(2, 0)
    y_last(3, 0)
    y_last(2, 1)

    @pl.when(s == 0)
    def _():
        for hh in (0, 1):
            wo_wait(hh * 2 + c)
            wo_share(hh).start()

    shared_wait(2)
    attend(2)
    y_last(3, 1)
    shared_wait(3)
    attend(3)
    for r in QUARTERS:
        rows = pl.ds(r * QUART, QUART)
        att[s, rows, :] = (oacc[rows, :] / den[rows, 0:1]).astype(BF16)
        att_copy(s, r).start()

    @pl.when(s == 0)
    def _():
        for hh in (0, 1):
            wo_wait(hh * 2 + 1 - c)

    @pl.when(s == 1)
    def _():
        wo_local().wait()

    load_res.wait()

    def chunk(o, g):
        rows = pl.ds(g * HALF, HALF)
        d = shard_of(o)
        block = wo[d // 2, pl.ds(pl.multiple_of((d % 2) * DH, DH), DH), :]
        pacc[o, rows, :] = lax.dot_general(
            att[0, rows, :], block[:, :DH], NT, preferred_element_type=F32
        ) + lax.dot_general(att[1, rows, :], block[:, DH:], NT, preferred_element_type=F32)

        @pl.when(jnp.logical_and(s == m // 4, d // 2 == m % 4))
        def _():
            columns = pl.ds(pl.multiple_of((d % 2) * DH, DH), DH)
            pacc[o, rows, :] += dres[rows, columns].astype(F32)

    def target(direction, distance):
        if distance == 0:
            return 0
        if distance == 4:
            return 7
        return 2 * distance - (0 if direction == "R" else 1)

    def rs_copy(direction, r, hop):
        k = (r * 2 + (direction == "L")) * 4 + hop
        return remote(sbuf.at[k], rbuf.at[k], rs_send.at[k], rs_recv.at[k], z_dev[direction])

    def rs_start(direction, r):
        k = (r * 2 + (direction == "L")) * 4
        sbuf[k] = pacc[target(direction, REACH[direction, r % 2]), pl.ds(r * QUART, QUART), :].astype(BF16)
        rs_copy(direction, r, 0).start()

    def rs_step(hop, *quarters):
        for r in quarters:
            for direction in ("R", "L") if r % 2 == 0 else ("L", "R"):
                reach = REACH[direction, r % 2]
                if hop < reach:
                    k = (r * 2 + (direction == "L")) * 4 + hop
                    rs_copy(direction, r, hop - 1).wait_recv()
                    own = pacc[target(direction, reach - hop), pl.ds(r * QUART, QUART), :]
                    sbuf[k] = (own + rbuf[k - 1].astype(F32)).astype(BF16)
                    rs_copy(direction, r, hop).start()

    for g in (0, 1):
        for r in (2 * g, 2 * g + 1):
            att_copy(1 - s, r).wait_recv()
        chunk(7, g)
        rs_start("R", 2 * g)
        rs_start("L", 2 * g + 1)
        chunk(5, g)
        rs_start("L", 2 * g)
        chunk(6, g)
        rs_start("R", 2 * g + 1)
    chunk(3, 0)
    chunk(4, 0)
    rs_step(1, 0, 1)
    chunk(3, 1)
    chunk(4, 1)
    rs_step(1, 2, 3)
    chunk(1, 0)
    chunk(2, 0)
    rs_step(2, 0, 1)
    chunk(1, 1)
    chunk(2, 1)
    rs_step(2, 2, 3)
    chunk(0, 0)
    rs_step(3, 0, 1)
    chunk(0, 1)
    rs_step(3, 2, 3)
    for r in QUARTERS:
        rows = pl.ds(r * QUART, QUART)
        total = pacc[0, rows, :]
        for direction in ("R", "L") if r % 2 else ("L", "R"):
            hop = REACH[direction, r % 2] - 1
            rs_copy(direction, r, hop).wait_recv()
            total = total + rbuf[(r * 2 + (direction == "L")) * 4 + hop].astype(F32)
        out[rows, :] = total.astype(BF16)

    for r in QUARTERS:
        for direction in ("R", "L"):
            for distance in range(1, REACH[direction, r % 2] + 1):
                z_copy(r, direction, distance).wait_send()
        for which in range(3, 17):
            kv_copy(kv.at[0, r], 0, r, which, partner).wait_send()

    @pl.when(s == 0)
    def _():
        for r in QUARTERS:
            for copy in x_copies(r):
                copy.wait_send()
        for hh in (0, 1):
            wo_share(hh).wait_send()

    @pl.when(s == 1)
    def _():
        for r in QUARTERS:
            q_copy(r).wait_send()
        for copy in wo_x_copies():
            copy.wait_send()

    for r in QUARTERS:
        att_copy(s, r).wait_send()
        for direction in ("R", "L"):
            for hop in range(REACH[direction, r % 2]):
                rs_copy(direction, r, hop).wait_send()


def local(enc_states, dec_states, section_weights, group_lengths):
    dma = pltpu.SemaphoreType.DMA
    vmem = pltpu.VMEM
    return pl.pallas_call(
        kernel,
        out_shape=jax.ShapeDtypeStruct((ROWS, DH), BF16),
        in_specs=[pl.BlockSpec(memory_space=pl.ANY)] * 3 + [pl.BlockSpec(memory_space=pltpu.SMEM)],
        out_specs=pl.BlockSpec(memory_space=pltpu.VMEM),
        scratch_shapes=[
            vmem((NZ, ROWS, FEAT), BF16),
            vmem((2, FEAT, 2, FEAT), BF16),
            vmem((NZ, FEAT, FEAT), BF16),
            vmem((NZ, FEAT, FEAT), BF16),
            vmem((4, FEAT, FEAT), BF16),
            vmem((2, ROWS, FEAT), F32),
            vmem((16, 4, BLOCK, DH), BF16),
            vmem((4, BLOCK, DH), BF16),
            vmem((ROWS, DH), BF16),
            vmem((ROWS, DH), BF16),
            vmem((ROWS, FEAT), BF16),
            vmem((2, ROWS, DH), BF16),
            vmem((ROWS, DH), F32),
            vmem((ROWS, 128), F32),
            vmem((ROWS, 128), F32),
            vmem((NZ, ROWS, DH), F32),
            vmem((32, QUART, DH), BF16),
            vmem((32, QUART, DH), BF16),
            dma((3,)),
            dma((2,)),
            dma((32,)),
            dma((32,)),
            dma((68,)),
            dma((64,)),
            dma((4,)),
            dma((4,)),
            dma((4,)),
            dma((4,)),
            dma((4,)),
            dma((4,)),
            dma((32,)),
            dma((32,)),
        ],
        compiler_params=pltpu.CompilerParams(
            collective_id=0, has_side_effects=True, vmem_limit_bytes=60 * 2**20
        ),
    )(enc_states, dec_states, section_weights, group_lengths)


def solution(mesh):
    in_specs = (P("seq", "mp"), P("seq", "mp"), P("segment", None, None, "mp"), P("seq"))
    out_specs = P("seq", ("segment", "mp"))
    return jax.shard_map(local, mesh=mesh, in_specs=in_specs, out_specs=out_specs, check_vma=False)
```

```python
import jax
import jax.numpy as jnp
from jax import lax
from jax.experimental import pallas as pl
from jax.experimental.pallas import tpu as pltpu
from jax.sharding import PartitionSpec as P

MESH = pl.DeviceIdType.MESH
F32, BF16 = jnp.float32, jnp.bfloat16
DH, GROUP = 256, 128
ROWS, FEAT, NZ = 256, 512, 8
HALF, QUART = ROWS // 2, ROWS // 4
BLOCK = 2 * (GROUP // 2) + 16
NEG = -1e30
DEINT = 32
OFFSETS = (0, -1, 1, -2, 2, -3, 3, 4)
REACH = {("R", 0): 4, ("R", 1): 3, ("L", 1): 4, ("L", 0): 3}
QUARTERS = (0, 1, 2, 3)
DIRECT = (2, 3)
NT = (((1,), (1,)), ((), ()))


def slot_of(direction, distance):
    if distance == 0:
        return 0
    if distance == 4:
        return 7
    return 2 * distance - (1 if direction == "R" else 0)


def kernel(enc, dec, weights, lengths, out, xg, stage, w0, w1, wo, acc, kv, ks, qbuf, qs, dres, att, oacc,
           mx, den, ps, psm, pr, prm, pacc, sbuf, rbuf, load_sem, stage_sem, z_send, z_recv, kv_send, kv_recv, q_send, q_recv,
           wo_send, wo_recv, p_send, p_recv, rs_send, rs_recv):
    s = lax.axis_index("segment")
    q = lax.axis_index("seq")
    m = lax.axis_index("mp")
    y, xh, c = q // 4, (q // 2) % 2, q % 2
    z_to = {"R": (m + 1) % NZ, "L": (m + NZ - 1) % NZ}

    def seq_of(yy, hh, cc):
        return (yy * 2 + hh) * 2 + cc

    y_up, y_down, y_far = (y + 1) % 4, (y + 3) % 4, (y + 2) % 4
    partner = (s, seq_of(y, xh, 1 - c), m)
    up, down = (s, seq_of(y_up, xh, c), m), (s, seq_of(y_down, xh, c), m)
    far = (s, seq_of(y_far, xh, c), m)
    across = (1 - s, q, m)
    across_other = (1 - s, seq_of(y, 1 - xh, c), m)
    same_other = (s, seq_of(y, 1 - xh, c), m)
    z_dev = {d: (s, q, z_to[d]) for d in ("R", "L")}

    def remote(src, dst, send, recv, device):
        return pltpu.make_async_remote_copy(
            src_ref=src, dst_ref=dst, send_sem=send, recv_sem=recv, device_id=device, device_id_type=MESH
        )

    def load_x(source):
        return pltpu.make_async_copy(source, xg.at[0], load_sem.at[0])

    @pl.when(s == 0)
    def _():
        load_x(enc).start()

    @pl.when(s == 1)
    def _():
        load_x(dec).start()

    load_res = pltpu.make_async_copy(dec, dres, load_sem.at[1])
    load_res.start()

    def shard_of(o):
        return (m + NZ + OFFSETS[o]) % NZ

    def stage_copy(o):
        rows = pl.ds(pl.multiple_of(shard_of(o) * FEAT, FEAT), FEAT)
        return pltpu.make_async_copy(weights.at[0, rows], stage.at[o % 2], stage_sem.at[o % 2])

    stage_copy(0).start()
    stage_copy(1).start()

    barrier = pltpu.get_barrier_semaphore()
    peers = (z_dev["R"], z_dev["L"], up, down, far, partner, across, across_other, same_other)
    for peer in peers:
        pl.semaphore_signal(barrier, inc=1, device_id=peer, device_id_type=MESH)
    pl.semaphore_wait(barrier, len(peers))

    def z_copy(r, direction, distance):
        rows = pl.ds(r * QUART, QUART)
        sems = (r * 2 + (direction == "L")) * 4 + distance - 1
        return remote(
            xg.at[slot_of(direction, distance - 1), rows],
            xg.at[slot_of(direction, distance), rows],
            z_send.at[sems],
            z_recv.at[sems],
            z_dev[direction],
        )

    def z_start(*quarters):
        for r in quarters:
            for direction in ("R", "L"):
                z_copy(r, direction, 1).start()

    def z_step(r, distance):
        for direction in ("R", "L"):
            reach = REACH[direction, r % 2]
            if distance <= reach:
                z_copy(r, direction, distance).wait_recv()
                if distance < reach:
                    z_copy(r, direction, distance + 1).start()

    def split(o):
        stage_copy(o).wait()
        j = shard_of(o)

        def body(i, carry):
            r = pl.multiple_of(i * DEINT, DEINT)
            pair = jnp.swapaxes(stage[o % 2, pl.ds(r, DEINT)], 0, 1)
            w0[o, pl.ds(r, DEINT), :] = pair[0]
            w1[j, pl.ds(r, DEINT), :] = pair[1]
            return carry

        lax.fori_loop(0, FEAT // DEINT, body, 0, unroll=2)
        if o + 2 < NZ:
            stage_copy(o + 2).start()

    def project(begin, end, o):
        rows = pl.ds(begin * QUART, (end - begin) * QUART)
        x = xg[o, rows, :]
        first = jnp.dot(x, w0[o], preferred_element_type=F32)
        if o == 0:
            acc[0, rows, :] = first
        else:
            acc[0, rows, :] += first

        @pl.when(s == 0)
        def _():
            second = jnp.dot(x, w1[shard_of(o)], preferred_element_type=F32)
            if o == 0:
                acc[1, rows, :] = second
            else:
                acc[1, rows, :] += second

    def kv_copy(src, index, r, which, device):
        return remote(src, kv.at[index, r], kv_send.at[r * 8 + which], kv_recv.at[r * 8 + index], device)

    def kv_wait(index, r):
        kv_copy(kv.at[index, r], index, r, 0, partner).wait_recv()

    def forward(index, r, which, device):
        kv_copy(kv.at[index, r], index, r, which, device).start()

    def x_copy(r):
        return kv_copy(ks.at[r], y * 2 + c, r, 0, across)

    def q_copies(r):
        rows = pl.ds(r * QUART, QUART)
        return (
            remote(qs.at[rows], qbuf.at[0, rows], q_send.at[r * 3], q_recv.at[r * 2], across),
            remote(qs.at[rows], qbuf.at[1, rows], q_send.at[r * 3 + 1], q_recv.at[r * 2 + 1], across_other),
            remote(qbuf.at[0, rows], qbuf.at[1, rows], q_send.at[r * 3 + 2], q_recv.at[r * 2 + 1], same_other),
        )

    def finish(r):
        rows = pl.ds(r * QUART, QUART)
        own = y * 2 + c

        @pl.when(s == 0)
        def _():
            lane = lax.broadcasted_iota(jnp.int32, (16, DH), 1) - c * QUART
            padding = jnp.logical_and(lane >= 0, lane + (r % 2) * QUART >= lengths[r // 2])
            bias = jnp.where(jnp.logical_and(padding, lane < QUART), NEG, 0.0).astype(BF16)
            ks[r, pl.ds(0, QUART), :] = acc[0, rows, DH:].astype(BF16)
            ks[r, pl.ds(QUART, QUART), :] = acc[1, rows, DH:].astype(BF16)
            ks[r, pl.ds(2 * QUART, 16), :] = bias
            x_copy(r).start()
            kv[own, r, pl.ds(0, QUART), :] = acc[0, rows, :DH].astype(BF16)
            kv[own, r, pl.ds(QUART, QUART), :] = acc[1, rows, :DH].astype(BF16)
            kv[own, r, pl.ds(2 * QUART, 16), :] = bias
            y_near(r, True)

        @pl.when(s == 1)
        def _():
            scale = DH ** -0.5
            qs[rows, :] = acc[0, rows, :DH].astype(BF16) * jnp.asarray(scale, BF16)
            qbuf[0, rows, :] = acc[0, rows, DH:].astype(BF16) * jnp.asarray(scale, BF16)
            for copy in q_copies(r):
                copy.start()

    def y_near(r, local_source):
        index = y * 2 + c
        if not local_source:
            kv_wait(index, r)
        if r in DIRECT:
            forward(index, r, 4, far)
        forward(index, r, 1, up)
        forward(index, r, 2, down)
        forward(index, r, 3, partner)

    def y_next(r):
        low, high = y_down * 2 + c, y_up * 2 + c
        one, other = ((low, up, 5, 6), high) if r % 2 == 0 else ((high, down, 6, 5), low)
        index, device, share_one, share_other = one
        kv_wait(index, r)
        if r not in DIRECT:
            forward(index, r, 4, device)
        forward(index, r, share_one, partner)
        kv_wait(other, r)
        forward(other, r, share_other, partner)

    def y_last(r):
        kv_wait(y_far * 2 + c, r)
        forward(y_far * 2 + c, r, 7, partner)

    def shared_wait(r):
        for yy in (y, y_down, y_up, y_far):
            kv_wait(yy * 2 + 1 - c, r)

    def attend(r, k):
        keys = jnp.concatenate([kv[b, r, pl.ds(0, QUART), :] for b in range(8)], axis=0)
        values = jnp.concatenate([kv[b, r, pl.ds(QUART, QUART), :] for b in range(8)], axis=0)
        signs = [kv[b, r, pl.ds(2 * QUART, 16), pl.ds(0, GROUP)].astype(F32)[0:1] for b in range(8)]
        bias = jnp.concatenate([signs[b] + signs[b + 1] for b in range(0, 8, 2)], axis=1)
        best, total = mx[k, :, 0:1], den[k, :, 0:1]
        scores = lax.dot_general(qbuf[k], keys, NT, preferred_element_type=F32) + bias
        new_best = jnp.maximum(best, jnp.max(scores, axis=1, keepdims=True))
        shrink = jnp.exp(best - new_best)
        probs = jnp.exp(scores - new_best).astype(BF16)
        mx[k] = jnp.broadcast_to(new_best, (ROWS, 128))
        den[k] = jnp.broadcast_to(total * shrink + jnp.sum(probs.astype(F32), axis=1, keepdims=True), (ROWS, 128))
        oacc[k] = oacc[k] * shrink + jnp.dot(probs, values, preferred_element_type=F32)

    def part_copies(k, g, device):
        rows = pl.ds(g * QUART, QUART)
        data = remote(ps.at[k, rows], pr.at[k, rows], p_send.at[k * 6 + g], p_recv.at[k * 6 + g], device)
        if g % 2:
            return (data,)
        n = k * 6 + 4 + g // 2
        return (remote(psm.at[k, g // 2], prm.at[k, g // 2], p_send.at[n], p_recv.at[n], device), data)

    def part_send(k):
        for g in QUARTERS:
            rows = pl.ds(g * QUART, QUART)
            ps[k, rows, :] = oacc[k, rows, :].astype(BF16)
            if g % 2 == 0:
                both = pl.ds(g * QUART, HALF)
                psm[k, g // 2, pl.ds(0, 8), :] = jnp.transpose(mx[k, both, :])[0:8]
                psm[k, g // 2, pl.ds(8, 8), :] = jnp.transpose(den[k, both, :])[0:8]
            for copy in part_copies(k, g, across if k == 0 else across_other):
                copy.start()

    def relay_copies(g):
        rows = pl.ds(g * QUART, QUART)
        data = remote(pr.at[1, rows], pr.at[2, rows], p_send.at[12 + g], p_recv.at[12 + g], across)
        if g % 2:
            return (data,)
        n = 16 + g // 2
        return (remote(prm.at[1, g // 2], prm.at[2, g // 2], p_send.at[n], p_recv.at[n], across), data)

    def column(row):
        return jnp.transpose(jnp.broadcast_to(row, (128, HALF)))[:, 0:1]

    def merge(head, g, one, one_best, one_sum, two, two_best, two_sum):
        best = jnp.maximum(one_best, two_best)
        one_share, two_share = jnp.exp(one_best - best), jnp.exp(two_best - best)
        scale = 1.0 / (one_sum * one_share + two_sum * two_share)
        att[head, pl.ds(g * HALF, HALF), :] = (one * (one_share * scale) + two * (two_share * scale)).astype(BF16)

    def received(slot, g):
        rows = pl.ds(g * HALF, HALF)
        return pr[slot, rows, :].astype(F32), column(prm[slot, g, 0:1, :]), column(prm[slot, g, 8:9, :])

    def part_wait(copies):
        for copy in copies:
            copy.wait_recv()

    part = xh * 2 + c

    def wo_x_copies():
        return (
            remote(w1.at[part], wo.at[part], wo_send.at[0], wo_recv.at[part], across),
            remote(w1.at[part], wo.at[part], wo_send.at[1], wo_recv.at[part], across_other),
        )

    def wo_share(hh):
        index = hh * 2 + c
        return remote(wo.at[index], wo.at[index], wo_send.at[2 + hh], wo_recv.at[index], partner)

    def wo_wait(index):
        remote(wo.at[index], wo.at[index], wo_send.at[0], wo_recv.at[index], partner).wait_recv()

    def wo_local():
        return pltpu.make_async_copy(w1.at[pl.ds(4, 4)], wo, load_sem.at[2])

    @pl.when(s == 0)
    def _():
        load_x(enc).wait()

    @pl.when(s == 1)
    def _():
        load_x(dec).wait()

    def enc_side(body, *args):
        @pl.when(s == 0)
        def _():
            body(*args)

    def dec_side(body, *args):
        @pl.when(s == 1)
        def _():
            body(*args)

    z_start(0, 1)
    mx[...] = jnp.full_like(mx, NEG)
    den[...] = jnp.zeros_like(den)
    oacc[...] = jnp.zeros_like(oacc)
    split(0)
    split(1)
    project(0, 2, 0)
    z_step(0, 1)
    z_step(1, 1)
    z_start(2, 3)
    split(2)
    split(3)
    project(0, 2, 1)
    project(0, 2, 2)
    z_step(0, 2)
    z_step(1, 2)
    split(4)
    split(5)
    project(0, 2, 3)
    project(0, 2, 4)
    z_step(2, 1)
    z_step(3, 1)
    split(6)
    split(7)

    @pl.when(s == 1)
    def _():
        for copy in wo_x_copies():
            copy.start()
        wo_local().start()

    z_step(0, 3)
    z_step(1, 3)
    z_step(2, 2)
    z_step(3, 2)
    project(0, 2, 5)
    project(0, 2, 6)
    z_step(0, 4)
    z_step(1, 4)
    project(0, 2, 7)
    finish(0)
    finish(1)
    project(2, 4, 0)
    project(2, 4, 1)
    project(2, 4, 2)
    project(2, 4, 3)
    z_step(2, 3)
    z_step(3, 3)
    project(2, 4, 4)
    project(2, 4, 5)
    project(2, 4, 6)
    dec_side(y_near, 0, False)
    dec_side(y_near, 1, False)
    z_step(2, 4)
    z_step(3, 4)
    project(2, 4, 7)
    finish(2)
    finish(3)
    y_next(0)
    dec_side(y_near, 2, False)
    y_next(1)
    dec_side(y_near, 3, False)
    y_next(2)
    y_last(0)
    y_last(1)
    for r in QUARTERS:
        q_copies(r)[1].wait_recv()

    @pl.when(s == 0)
    def _():
        for r in QUARTERS:
            q_copies(r)[0].wait_recv()

    shared_wait(0)
    attend(0, 1)
    attend(0, 0)
    y_next(3)
    shared_wait(1)
    attend(1, 1)
    y_last(2)
    attend(1, 0)
    y_last(3)
    shared_wait(2)
    attend(2, 1)
    attend(2, 0)

    @pl.when(s == 0)
    def _():
        for hh in (0, 1):
            wo_wait(hh * 2 + c)
            wo_share(hh).start()

    shared_wait(3)
    attend(3, 1)
    part_send(1)
    attend(3, 0)
    part_send(0)

    @pl.when(s == 0)
    def _():
        for hh in (0, 1):
            wo_wait(hh * 2 + 1 - c)

    @pl.when(s == 1)
    def _():
        wo_local().wait()

    load_res.wait()

    def chunk(o, g):
        rows = pl.ds(g * HALF, HALF)
        d = shard_of(o)
        block = wo[d // 2, pl.ds(pl.multiple_of((d % 2) * DH, DH), DH), :]
        pacc[o, rows, :] = lax.dot_general(
            att[0, rows, :], block[:, :DH], NT, preferred_element_type=F32
        ) + lax.dot_general(att[1, rows, :], block[:, DH:], NT, preferred_element_type=F32)

        @pl.when(jnp.logical_and(s == m // 4, d // 2 == m % 4))
        def _():
            columns = pl.ds(pl.multiple_of((d % 2) * DH, DH), DH)
            pacc[o, rows, :] += dres[rows, columns].astype(F32)

    def target(direction, distance):
        if distance == 0:
            return 0
        if distance == 4:
            return 7
        return 2 * distance - (0 if direction == "R" else 1)

    def rs_copy(direction, r, hop):
        k = (r * 2 + (direction == "L")) * 4 + hop
        return remote(sbuf.at[k], rbuf.at[k], rs_send.at[k], rs_recv.at[k], z_dev[direction])

    def rs_start(direction, r):
        k = (r * 2 + (direction == "L")) * 4
        sbuf[k] = pacc[target(direction, REACH[direction, r % 2]), pl.ds(r * QUART, QUART), :].astype(BF16)
        rs_copy(direction, r, 0).start()

    def rs_step(hop, *quarters):
        for r in quarters:
            for direction in ("R", "L") if r % 2 == 0 else ("L", "R"):
                reach = REACH[direction, r % 2]
                if hop < reach:
                    k = (r * 2 + (direction == "L")) * 4 + hop
                    rs_copy(direction, r, hop - 1).wait_recv()
                    own = pacc[target(direction, reach - hop), pl.ds(r * QUART, QUART), :]
                    sbuf[k] = (own + rbuf[k - 1].astype(F32)).astype(BF16)
                    rs_copy(direction, r, hop).start()

    def relay(g):
        part_wait(part_copies(1, g, across_other))
        for copy in relay_copies(g):
            copy.start()

    def gather(g):
        for r in (2 * g, 2 * g + 1):
            part_wait(part_copies(0, r, across))
        merge(1 - s, g, *received(0, g), *received(1, g))
        for r in (2 * g, 2 * g + 1):
            part_wait(relay_copies(r))
        rows = pl.ds(g * HALF, HALF)
        merge(s, g, oacc[0, rows, :], mx[0, rows, 0:1], den[0, rows, 0:1], *received(2, g))

    for g in QUARTERS:
        relay(g)
    for g in (0, 1):
        gather(g)
        chunk(7, g)
        rs_start("R", 2 * g)
        rs_start("L", 2 * g + 1)
        chunk(5, g)
        rs_start("L", 2 * g)
        chunk(6, g)
        rs_start("R", 2 * g + 1)
    chunk(3, 0)
    chunk(4, 0)
    rs_step(1, 0, 1)
    chunk(3, 1)
    chunk(4, 1)
    rs_step(1, 2, 3)
    chunk(1, 0)
    chunk(2, 0)
    rs_step(2, 0, 1)
    chunk(1, 1)
    chunk(2, 1)
    rs_step(2, 2, 3)
    chunk(0, 0)
    rs_step(3, 0, 1)
    chunk(0, 1)
    rs_step(3, 2, 3)
    for r in QUARTERS:
        rows = pl.ds(r * QUART, QUART)
        total = pacc[0, rows, :]
        for direction in ("R", "L") if r % 2 else ("L", "R"):
            hop = REACH[direction, r % 2] - 1
            rs_copy(direction, r, hop).wait_recv()
            total = total + rbuf[(r * 2 + (direction == "L")) * 4 + hop].astype(F32)
        out[rows, :] = total.astype(BF16)

    for r in QUARTERS:
        for direction in ("R", "L"):
            for distance in range(1, REACH[direction, r % 2] + 1):
                z_copy(r, direction, distance).wait_send()
        for which in range(1, 8):
            kv_copy(kv.at[0, r], 0, r, which, partner).wait_send()

    @pl.when(s == 0)
    def _():
        for r in QUARTERS:
            x_copy(r).wait_send()
        for hh in (0, 1):
            wo_share(hh).wait_send()

    @pl.when(s == 1)
    def _():
        for r in QUARTERS:
            for copy in q_copies(r):
                copy.wait_send()
        for copy in wo_x_copies():
            copy.wait_send()

    for r in QUARTERS:
        for copy in (*part_copies(0, r, across), *part_copies(1, r, across_other), *relay_copies(r)):
            copy.wait_send()
        for direction in ("R", "L"):
            for hop in range(REACH[direction, r % 2]):
                rs_copy(direction, r, hop).wait_send()


def local(enc_states, dec_states, section_weights, group_lengths):
    dma = pltpu.SemaphoreType.DMA
    vmem = pltpu.VMEM
    return pl.pallas_call(
        kernel,
        out_shape=jax.ShapeDtypeStruct((ROWS, DH), BF16),
        in_specs=[pl.BlockSpec(memory_space=pl.ANY)] * 3 + [pl.BlockSpec(memory_space=pltpu.SMEM)],
        out_specs=pl.BlockSpec(memory_space=pltpu.VMEM),
        scratch_shapes=[
            vmem((NZ, ROWS, FEAT), BF16),
            vmem((2, FEAT, 2, FEAT), BF16),
            vmem((NZ, FEAT, FEAT), BF16),
            vmem((NZ, FEAT, FEAT), BF16),
            vmem((4, FEAT, FEAT), BF16),
            vmem((2, ROWS, FEAT), F32),
            vmem((8, 4, BLOCK, DH), BF16),
            vmem((4, BLOCK, DH), BF16),
            vmem((2, ROWS, DH), BF16),
            vmem((ROWS, DH), BF16),
            vmem((ROWS, FEAT), BF16),
            vmem((2, ROWS, DH), BF16),
            vmem((2, ROWS, DH), F32),
            vmem((2, ROWS, 128), F32),
            vmem((2, ROWS, 128), F32),
            vmem((2, ROWS, DH), BF16),
            vmem((2, 2, 16, HALF), F32),
            vmem((3, ROWS, DH), BF16),
            vmem((3, 2, 16, HALF), F32),
            vmem((NZ, ROWS, DH), F32),
            vmem((32, QUART, DH), BF16),
            vmem((32, QUART, DH), BF16),
            dma((3,)),
            dma((2,)),
            dma((32,)),
            dma((32,)),
            dma((32,)),
            dma((32,)),
            dma((12,)),
            dma((8,)),
            dma((4,)),
            dma((4,)),
            dma((18,)),
            dma((18,)),
            dma((32,)),
            dma((32,)),
        ],
        compiler_params=pltpu.CompilerParams(
            collective_id=0, has_side_effects=True, vmem_limit_bytes=60 * 2**20
        ),
    )(enc_states, dec_states, section_weights, group_lengths)


def solution(mesh):
    in_specs = (P("seq", "mp"), P("seq", "mp"), P("segment", None, None, "mp"), P("seq"))
    out_specs = P("seq", ("segment", "mp"))
    return jax.shard_map(local, mesh=mesh, in_specs=in_specs, out_specs=out_specs, check_vma=False)
```

```python
import jax
import jax.numpy as jnp
from jax import lax
from jax.experimental import pallas as pl
from jax.experimental.pallas import tpu as pltpu
from jax.sharding import PartitionSpec as P

MESH = pl.DeviceIdType.MESH
F32, BF16 = jnp.float32, jnp.bfloat16
DH, GROUP = 256, 128
ROWS, FEAT, NZ = 256, 512, 8
HALF, QUART = ROWS // 2, ROWS // 4
BLOCK = 2 * (GROUP // 2) + 16
NEG = -1e30
DEINT = 32
OFFSETS = (0, -1, 1, -2, 2, -3, 3, 4)
REACH = {("R", 0): 4, ("R", 1): 3, ("L", 1): 4, ("L", 0): 3}
QUARTERS = (0, 1, 2, 3)
DIRECT = (2, 3)
NT = (((1,), (1,)), ((), ()))


def slot_of(direction, distance):
    if distance == 0:
        return 0
    if distance == 4:
        return 7
    return 2 * distance - (1 if direction == "R" else 0)


def kernel(enc, dec, weights, lengths, out, xg, stage, w0, w1, wo, acc, kv, ks, qbuf, qs, dres, att, oacc,
           mx, den, ps, psm, pr, prm, pacc, sbuf, rbuf, load_sem, stage_sem, z_send, z_recv, kv_send, kv_recv, q_send, q_recv,
           wo_send, wo_recv, p_send, p_recv, rs_send, rs_recv):
    s = lax.axis_index("segment")
    q = lax.axis_index("seq")
    m = lax.axis_index("mp")
    y, xh, c = q // 4, (q // 2) % 2, q % 2
    z_to = {"R": (m + 1) % NZ, "L": (m + NZ - 1) % NZ}

    def seq_of(yy, hh, cc):
        return (yy * 2 + hh) * 2 + cc

    y_up, y_down, y_far = (y + 1) % 4, (y + 3) % 4, (y + 2) % 4
    partner = (s, seq_of(y, xh, 1 - c), m)
    up, down = (s, seq_of(y_up, xh, c), m), (s, seq_of(y_down, xh, c), m)
    far = (s, seq_of(y_far, xh, c), m)
    across = (1 - s, q, m)
    across_other = (1 - s, seq_of(y, 1 - xh, c), m)
    same_other = (s, seq_of(y, 1 - xh, c), m)
    z_dev = {d: (s, q, z_to[d]) for d in ("R", "L")}

    def remote(src, dst, send, recv, device):
        return pltpu.make_async_remote_copy(
            src_ref=src, dst_ref=dst, send_sem=send, recv_sem=recv, device_id=device, device_id_type=MESH
        )

    def load_x(source):
        return pltpu.make_async_copy(source, xg.at[0], load_sem.at[0])

    @pl.when(s == 0)
    def _():
        load_x(enc).start()

    @pl.when(s == 1)
    def _():
        load_x(dec).start()

    load_res = pltpu.make_async_copy(dec, dres, load_sem.at[1])
    load_res.start()

    def shard_of(o):
        return (m + NZ + OFFSETS[o]) % NZ

    def stage_copy(o):
        rows = pl.ds(pl.multiple_of(shard_of(o) * FEAT, FEAT), FEAT)
        return pltpu.make_async_copy(weights.at[0, rows], stage.at[o % 2], stage_sem.at[o % 2])

    stage_copy(0).start()
    stage_copy(1).start()

    barrier = pltpu.get_barrier_semaphore()
    peers = (z_dev["R"], z_dev["L"], up, down, far, partner, across, across_other, same_other)
    for peer in peers:
        pl.semaphore_signal(barrier, inc=1, device_id=peer, device_id_type=MESH)
    pl.semaphore_wait(barrier, len(peers))

    def z_copy(r, direction, distance):
        rows = pl.ds(r * QUART, QUART)
        sems = (r * 2 + (direction == "L")) * 4 + distance - 1
        return remote(
            xg.at[slot_of(direction, distance - 1), rows],
            xg.at[slot_of(direction, distance), rows],
            z_send.at[sems],
            z_recv.at[sems],
            z_dev[direction],
        )

    def z_start(*quarters):
        for r in quarters:
            for direction in ("R", "L"):
                z_copy(r, direction, 1).start()

    def z_step(r, distance):
        for direction in ("R", "L"):
            reach = REACH[direction, r % 2]
            if distance <= reach:
                z_copy(r, direction, distance).wait_recv()
                if distance < reach:
                    z_copy(r, direction, distance + 1).start()

    def split(o):
        stage_copy(o).wait()
        j = shard_of(o)

        def body(i, carry):
            r = pl.multiple_of(i * DEINT, DEINT)
            pair = jnp.swapaxes(stage[o % 2, pl.ds(r, DEINT)], 0, 1)
            w0[o, pl.ds(r, DEINT), :] = pair[0]
            w1[j, pl.ds(r, DEINT), :] = pair[1]
            return carry

        lax.fori_loop(0, FEAT // DEINT, body, 0, unroll=2)
        if o + 2 < NZ:
            stage_copy(o + 2).start()

    def project(begin, end, o):
        rows = pl.ds(begin * QUART, (end - begin) * QUART)
        x = xg[o, rows, :]
        first = jnp.dot(x, w0[o], preferred_element_type=F32)
        if o == 0:
            acc[0, rows, :] = first
        else:
            acc[0, rows, :] += first

        @pl.when(s == 0)
        def _():
            second = jnp.dot(x, w1[shard_of(o)], preferred_element_type=F32)
            if o == 0:
                acc[1, rows, :] = second
            else:
                acc[1, rows, :] += second

    def kv_copy(src, index, r, which, device):
        return remote(src, kv.at[index, r], kv_send.at[r * 8 + which], kv_recv.at[r * 8 + index], device)

    def kv_wait(index, r):
        kv_copy(kv.at[index, r], index, r, 0, partner).wait_recv()

    def forward(index, r, which, device):
        kv_copy(kv.at[index, r], index, r, which, device).start()

    def x_copy(r):
        return kv_copy(ks.at[r], y * 2 + c, r, 0, across)

    def q_copies(r):
        rows = pl.ds(r * QUART, QUART)
        return (
            remote(qs.at[rows], qbuf.at[0, rows], q_send.at[r * 3], q_recv.at[r * 2], across),
            remote(qs.at[rows], qbuf.at[1, rows], q_send.at[r * 3 + 1], q_recv.at[r * 2 + 1], across_other),
            remote(qbuf.at[0, rows], qbuf.at[1, rows], q_send.at[r * 3 + 2], q_recv.at[r * 2 + 1], same_other),
        )

    def finish(r):
        rows = pl.ds(r * QUART, QUART)
        own = y * 2 + c

        @pl.when(s == 0)
        def _():
            lane = lax.broadcasted_iota(jnp.int32, (16, DH), 1) - c * QUART
            padding = jnp.logical_and(lane >= 0, lane + (r % 2) * QUART >= lengths[r // 2])
            bias = jnp.where(jnp.logical_and(padding, lane < QUART), NEG, 0.0).astype(BF16)
            ks[r, pl.ds(0, QUART), :] = acc[0, rows, DH:].astype(BF16)
            ks[r, pl.ds(QUART, QUART), :] = acc[1, rows, DH:].astype(BF16)
            ks[r, pl.ds(2 * QUART, 16), :] = bias
            x_copy(r).start()
            kv[own, r, pl.ds(0, QUART), :] = acc[0, rows, :DH].astype(BF16)
            kv[own, r, pl.ds(QUART, QUART), :] = acc[1, rows, :DH].astype(BF16)
            kv[own, r, pl.ds(2 * QUART, 16), :] = bias
            y_near(r, True)

        @pl.when(s == 1)
        def _():
            scale = DH ** -0.5
            qs[rows, :] = acc[0, rows, :DH].astype(BF16) * jnp.asarray(scale, BF16)
            qbuf[0, rows, :] = acc[0, rows, DH:].astype(BF16) * jnp.asarray(scale, BF16)
            for copy in q_copies(r):
                copy.start()

    def y_near(r, local_source):
        index = y * 2 + c
        if not local_source:
            kv_wait(index, r)
        if r in DIRECT:
            forward(index, r, 4, far)
        forward(index, r, 1, up)
        forward(index, r, 2, down)
        forward(index, r, 3, partner)

    def y_next(r):
        low, high = y_down * 2 + c, y_up * 2 + c
        one, other = ((low, up, 5, 6), high) if r % 2 == 0 else ((high, down, 6, 5), low)
        index, device, share_one, share_other = one
        kv_wait(index, r)
        if r not in DIRECT:
            forward(index, r, 4, device)
        forward(index, r, share_one, partner)
        kv_wait(other, r)
        forward(other, r, share_other, partner)

    def y_last(r):
        kv_wait(y_far * 2 + c, r)
        forward(y_far * 2 + c, r, 7, partner)

    def shared_wait(r):
        for yy in (y, y_down, y_up, y_far):
            kv_wait(yy * 2 + 1 - c, r)

    def attend(r, k):
        keys = jnp.concatenate([kv[b, r, pl.ds(0, QUART), :] for b in range(8)], axis=0)
        values = jnp.concatenate([kv[b, r, pl.ds(QUART, QUART), :] for b in range(8)], axis=0)
        signs = [kv[b, r, pl.ds(2 * QUART, 16), pl.ds(0, GROUP)].astype(F32)[0:1] for b in range(8)]
        bias = jnp.concatenate([signs[b] + signs[b + 1] for b in range(0, 8, 2)], axis=1)
        best, total = mx[k, :, 0:1], den[k, :, 0:1]
        scores = lax.dot_general(qbuf[k], keys, NT, preferred_element_type=F32) + bias
        new_best = jnp.maximum(best, jnp.max(scores, axis=1, keepdims=True))
        shrink = jnp.exp(best - new_best)
        probs = jnp.exp(scores - new_best).astype(BF16)
        mx[k] = jnp.broadcast_to(new_best, (ROWS, 128))
        den[k] = jnp.broadcast_to(total * shrink + jnp.sum(probs.astype(F32), axis=1, keepdims=True), (ROWS, 128))
        oacc[k] = oacc[k] * shrink + jnp.dot(probs, values, preferred_element_type=F32)

    def part_copies(k, g, device):
        rows = pl.ds(g * QUART, QUART)
        data = remote(ps.at[k, rows], pr.at[k, rows], p_send.at[k * 6 + g], p_recv.at[k * 6 + g], device)
        if g % 2:
            return (data,)
        n = k * 6 + 4 + g // 2
        return (remote(psm.at[k, g // 2], prm.at[k, g // 2], p_send.at[n], p_recv.at[n], device), data)

    def part_send(k):
        for g in QUARTERS:
            rows = pl.ds(g * QUART, QUART)
            ps[k, rows, :] = oacc[k, rows, :].astype(BF16)
            if g % 2 == 0:
                both = pl.ds(g * QUART, HALF)
                psm[k, g // 2, pl.ds(0, 8), :] = jnp.transpose(mx[k, both, :])[0:8]
                psm[k, g // 2, pl.ds(8, 8), :] = jnp.transpose(den[k, both, :])[0:8]
            for copy in part_copies(k, g, across if k == 0 else across_other):
                copy.start()

    def relay_copies(g):
        rows = pl.ds(g * QUART, QUART)
        data = remote(pr.at[1, rows], pr.at[2, rows], p_send.at[12 + g], p_recv.at[12 + g], across)
        if g % 2:
            return (data,)
        n = 16 + g // 2
        return (remote(prm.at[1, g // 2], prm.at[2, g // 2], p_send.at[n], p_recv.at[n], across), data)

    def column(row):
        return jnp.transpose(jnp.broadcast_to(row, (128, HALF)))[:, 0:1]

    def merge(head, g, one, one_best, one_sum, two, two_best, two_sum):
        best = jnp.maximum(one_best, two_best)
        one_share, two_share = jnp.exp(one_best - best), jnp.exp(two_best - best)
        scale = 1.0 / (one_sum * one_share + two_sum * two_share)
        att[head, pl.ds(g * HALF, HALF), :] = (one * (one_share * scale) + two * (two_share * scale)).astype(BF16)

    def received(slot, g):
        rows = pl.ds(g * HALF, HALF)
        return pr[slot, rows, :].astype(F32), column(prm[slot, g, 0:1, :]), column(prm[slot, g, 8:9, :])

    def part_wait(copies):
        for copy in copies:
            copy.wait_recv()

    part = xh * 2 + c

    def wo_x_copies():
        return (
            remote(w1.at[part], wo.at[part], wo_send.at[0], wo_recv.at[part], across),
            remote(w1.at[part], wo.at[part], wo_send.at[1], wo_recv.at[part], across_other),
        )

    def wo_share(hh):
        index = hh * 2 + c
        return remote(wo.at[index], wo.at[index], wo_send.at[2 + hh], wo_recv.at[index], partner)

    def wo_wait(index):
        remote(wo.at[index], wo.at[index], wo_send.at[0], wo_recv.at[index], partner).wait_recv()

    def wo_local():
        return pltpu.make_async_copy(w1.at[pl.ds(4, 4)], wo, load_sem.at[2])

    @pl.when(s == 0)
    def _():
        load_x(enc).wait()

    @pl.when(s == 1)
    def _():
        load_x(dec).wait()

    def enc_side(body, *args):
        @pl.when(s == 0)
        def _():
            body(*args)

    def dec_side(body, *args):
        @pl.when(s == 1)
        def _():
            body(*args)

    z_start(0, 1)
    mx[...] = jnp.full_like(mx, NEG)
    den[...] = jnp.zeros_like(den)
    oacc[...] = jnp.zeros_like(oacc)
    split(0)
    split(1)
    project(0, 2, 0)
    z_step(0, 1)
    z_step(1, 1)
    z_start(2, 3)
    split(2)
    split(3)
    project(0, 2, 1)
    project(0, 2, 2)
    z_step(0, 2)
    z_step(1, 2)
    split(4)
    split(5)
    project(0, 2, 3)
    project(0, 2, 4)
    z_step(2, 1)
    z_step(3, 1)
    split(6)
    split(7)

    @pl.when(s == 1)
    def _():
        for copy in wo_x_copies():
            copy.start()
        wo_local().start()

    z_step(0, 3)
    z_step(1, 3)
    z_step(2, 2)
    z_step(3, 2)
    project(0, 2, 5)
    project(0, 2, 6)
    z_step(0, 4)
    z_step(1, 4)
    project(0, 2, 7)
    finish(0)
    finish(1)
    project(2, 4, 0)
    project(2, 4, 1)
    project(2, 4, 2)
    project(2, 4, 3)
    z_step(2, 3)
    z_step(3, 3)
    project(2, 4, 4)
    project(2, 4, 5)
    project(2, 4, 6)
    dec_side(y_near, 0, False)
    dec_side(y_near, 1, False)
    z_step(2, 4)
    z_step(3, 4)
    project(2, 4, 7)
    finish(2)
    finish(3)
    y_next(0)
    dec_side(y_near, 2, False)
    y_next(1)
    dec_side(y_near, 3, False)
    y_next(2)
    y_last(0)
    y_last(1)
    for r in QUARTERS:
        q_copies(r)[1].wait_recv()

    @pl.when(s == 0)
    def _():
        for r in QUARTERS:
            q_copies(r)[0].wait_recv()

    shared_wait(0)
    attend(0, 1)
    attend(0, 0)
    y_next(3)
    shared_wait(1)
    attend(1, 1)
    y_last(2)
    attend(1, 0)
    y_last(3)
    shared_wait(2)
    attend(2, 1)

    @pl.when(s == 0)
    def _():
        for hh in (0, 1):
            wo_wait(hh * 2 + c)
            wo_share(hh).start()

    shared_wait(3)
    attend(3, 1)
    part_send(1)
    attend(2, 0)
    attend(3, 0)
    part_send(0)

    @pl.when(s == 0)
    def _():
        for hh in (0, 1):
            wo_wait(hh * 2 + 1 - c)

    @pl.when(s == 1)
    def _():
        wo_local().wait()

    load_res.wait()

    def chunk(o, g):
        rows = pl.ds(g * HALF, HALF)
        d = shard_of(o)
        block = wo[d // 2, pl.ds(pl.multiple_of((d % 2) * DH, DH), DH), :]
        pacc[o, rows, :] = lax.dot_general(
            att[0, rows, :], block[:, :DH], NT, preferred_element_type=F32
        ) + lax.dot_general(att[1, rows, :], block[:, DH:], NT, preferred_element_type=F32)

        @pl.when(jnp.logical_and(s == m // 4, d // 2 == m % 4))
        def _():
            columns = pl.ds(pl.multiple_of((d % 2) * DH, DH), DH)
            pacc[o, rows, :] += dres[rows, columns].astype(F32)

    def target(direction, distance):
        if distance == 0:
            return 0
        if distance == 4:
            return 7
        return 2 * distance - (0 if direction == "R" else 1)

    def rs_copy(direction, r, hop):
        k = (r * 2 + (direction == "L")) * 4 + hop
        return remote(sbuf.at[k], rbuf.at[k], rs_send.at[k], rs_recv.at[k], z_dev[direction])

    def rs_start(direction, r):
        k = (r * 2 + (direction == "L")) * 4
        sbuf[k] = pacc[target(direction, REACH[direction, r % 2]), pl.ds(r * QUART, QUART), :].astype(BF16)
        rs_copy(direction, r, 0).start()

    def rs_step(hop, *quarters):
        for r in quarters:
            for direction in ("R", "L") if r % 2 == 0 else ("L", "R"):
                reach = REACH[direction, r % 2]
                if hop < reach:
                    k = (r * 2 + (direction == "L")) * 4 + hop
                    rs_copy(direction, r, hop - 1).wait_recv()
                    own = pacc[target(direction, reach - hop), pl.ds(r * QUART, QUART), :]
                    sbuf[k] = (own + rbuf[k - 1].astype(F32)).astype(BF16)
                    rs_copy(direction, r, hop).start()

    def relay(g):
        part_wait(part_copies(1, g, across_other))
        for copy in relay_copies(g):
            copy.start()

    def gather(g):
        for r in (2 * g, 2 * g + 1):
            part_wait(part_copies(0, r, across))
        merge(1 - s, g, *received(0, g), *received(1, g))
        for r in (2 * g, 2 * g + 1):
            part_wait(relay_copies(r))
        rows = pl.ds(g * HALF, HALF)
        merge(s, g, oacc[0, rows, :], mx[0, rows, 0:1], den[0, rows, 0:1], *received(2, g))

    for g in QUARTERS:
        relay(g)
    for g in (0, 1):
        gather(g)
        chunk(7, g)
        rs_start("R", 2 * g)
        rs_start("L", 2 * g + 1)
        chunk(5, g)
        rs_start("L", 2 * g)
        chunk(6, g)
        rs_start("R", 2 * g + 1)
    chunk(3, 0)
    chunk(4, 0)
    rs_step(1, 0, 1)
    chunk(3, 1)
    chunk(4, 1)
    rs_step(1, 2, 3)
    chunk(1, 0)
    chunk(2, 0)
    rs_step(2, 0, 1)
    chunk(1, 1)
    chunk(2, 1)
    rs_step(2, 2, 3)
    chunk(0, 0)
    rs_step(3, 0, 1)
    chunk(0, 1)
    rs_step(3, 2, 3)
    for r in QUARTERS:
        rows = pl.ds(r * QUART, QUART)
        total = pacc[0, rows, :]
        for direction in ("R", "L") if r % 2 else ("L", "R"):
            hop = REACH[direction, r % 2] - 1
            rs_copy(direction, r, hop).wait_recv()
            total = total + rbuf[(r * 2 + (direction == "L")) * 4 + hop].astype(F32)
        out[rows, :] = total.astype(BF16)

    for r in QUARTERS:
        for direction in ("R", "L"):
            for distance in range(1, REACH[direction, r % 2] + 1):
                z_copy(r, direction, distance).wait_send()
        for which in range(1, 8):
            kv_copy(kv.at[0, r], 0, r, which, partner).wait_send()

    @pl.when(s == 0)
    def _():
        for r in QUARTERS:
            x_copy(r).wait_send()
        for hh in (0, 1):
            wo_share(hh).wait_send()

    @pl.when(s == 1)
    def _():
        for r in QUARTERS:
            for copy in q_copies(r):
                copy.wait_send()
        for copy in wo_x_copies():
            copy.wait_send()

    for r in QUARTERS:
        for copy in (*part_copies(0, r, across), *part_copies(1, r, across_other), *relay_copies(r)):
            copy.wait_send()
        for direction in ("R", "L"):
            for hop in range(REACH[direction, r % 2]):
                rs_copy(direction, r, hop).wait_send()


def local(enc_states, dec_states, section_weights, group_lengths):
    dma = pltpu.SemaphoreType.DMA
    vmem = pltpu.VMEM
    return pl.pallas_call(
        kernel,
        out_shape=jax.ShapeDtypeStruct((ROWS, DH), BF16),
        in_specs=[pl.BlockSpec(memory_space=pl.ANY)] * 3 + [pl.BlockSpec(memory_space=pltpu.SMEM)],
        out_specs=pl.BlockSpec(memory_space=pltpu.VMEM),
        scratch_shapes=[
            vmem((NZ, ROWS, FEAT), BF16),
            vmem((2, FEAT, 2, FEAT), BF16),
            vmem((NZ, FEAT, FEAT), BF16),
            vmem((NZ, FEAT, FEAT), BF16),
            vmem((4, FEAT, FEAT), BF16),
            vmem((2, ROWS, FEAT), F32),
            vmem((8, 4, BLOCK, DH), BF16),
            vmem((4, BLOCK, DH), BF16),
            vmem((2, ROWS, DH), BF16),
            vmem((ROWS, DH), BF16),
            vmem((ROWS, FEAT), BF16),
            vmem((2, ROWS, DH), BF16),
            vmem((2, ROWS, DH), F32),
            vmem((2, ROWS, 128), F32),
            vmem((2, ROWS, 128), F32),
            vmem((2, ROWS, DH), BF16),
            vmem((2, 2, 16, HALF), F32),
            vmem((3, ROWS, DH), BF16),
            vmem((3, 2, 16, HALF), F32),
            vmem((NZ, ROWS, DH), F32),
            vmem((32, QUART, DH), BF16),
            vmem((32, QUART, DH), BF16),
            dma((3,)),
            dma((2,)),
            dma((32,)),
            dma((32,)),
            dma((32,)),
            dma((32,)),
            dma((12,)),
            dma((8,)),
            dma((4,)),
            dma((4,)),
            dma((18,)),
            dma((18,)),
            dma((32,)),
            dma((32,)),
        ],
        compiler_params=pltpu.CompilerParams(
            collective_id=0, has_side_effects=True, vmem_limit_bytes=60 * 2**20
        ),
    )(enc_states, dec_states, section_weights, group_lengths)


def solution(mesh):
    in_specs = (P("seq", "mp"), P("seq", "mp"), P("segment", None, None, "mp"), P("seq"))
    out_specs = P("seq", ("segment", "mp"))
    return jax.shard_map(local, mesh=mesh, in_specs=in_specs, out_specs=out_specs, check_vma=False)
```
